256 devices in a mesh: grp: 2 (over core), row: 8 (over y, z_lo), col: 16 (over x, z_hi).
Axes of the slice: x: 4, y: 4, z: 8 (z_hi: 4, z_lo: 2; z = z_hi * 2 + z_lo), core: 2. Of those that a mesh axis runs over, the one named last changes fastest.
Arguments:
- load: float32 [16, 16, 1024, 256], P(('grp', 'row'), 'col'), may hold values from -6 to 6
- guess: float32 [16, 16, 1024, 256], P(('grp', 'row'), 'col'), may hold values from -6 to 6
- interface_op: bfloat16 [16, 16, 1024, 1024], P(('grp', 'row'), 'col'), may hold values from -1 to 5
- precond: bfloat16 [16, 16, 1024, 1024], P(('grp', 'row'), 'col'), may hold values from -1 to 2
- basis: bfloat16 [16, 16, 1024, 64], P(('grp', 'row'), 'col'), may hold values from -0.375 to 0.375
- coarse_inverse: bfloat16 [16384, 16384], P(('grp', 'row'), 'col'), may hold values from -0.0625 to 0.0625
- edge_rows: int32 [16, 16, 1024], P(('grp', 'row'), 'col'), may hold values from 0 to 1023, each once within a row
- coarse_slot: int32 [16, 16, 64], P(('grp', 'row'), 'col'), may hold values from 0 to 63, each once within a row
Outputs:
- displacement: float32 [16, 16, 1024, 256], P(('grp', 'row'), 'col')
The draws below stay inside these ranges and needn't reach their ends.
Inputs may be any that keep to these rules, and one draw needn't show every extreme that they name: `edge_rows`: each subdomain lists each of its 1024 interface rows once. `coarse_slot`: each subdomain gives each of its 64 basis vectors a different offset.
All inputs are finite; a program needn't handle non-finite values.
Results may differ from the reference program's by a relative error of at most 0.0095.
Values may be sent and summed in bfloat16 or wider, within the bound.
A program may use at most 64 MiB of HBM per device.

```python
import math
import jax
import jax.numpy as jnp
from jax import lax

NI = 1024
NB = 64
R = 256
ITERS = 2
GRID_R = 16
GRID_C = 16
COARSE = 16384


def dominant_matrix(key, off_scale, diag_lo, diag_hi):
    first, second = jax.random.split(key)
    shape = (GRID_R, GRID_C, NI, NI)
    coupling = jax.random.truncated_normal(first, -4.0, 4.0, shape, jnp.float32)
    diagonal = jax.random.uniform(second, (GRID_R, GRID_C, NI), jnp.float32, diag_lo, diag_hi)
    matrix = coupling * (off_scale / math.sqrt(NI)) + diagonal[..., None] * jnp.eye(NI, dtype=jnp.float32)
    return matrix.astype(jnp.bfloat16)


def draw_interface_op(key, part):
    return dominant_matrix(jax.random.fold_in(key, 11), 0.6, 1.0, 3.0)


def draw_precond(key, part):
    return dominant_matrix(jax.random.fold_in(key, 23), 0.15, 0.3, 0.9)


def with_spikes(values, rng, source, target, shards_of, factor):
    owner, partner = [(jnp.arange(values.shape[axis_at]) // (values.shape[axis_at] // shards_of)).reshape([-1 if axis == axis_at else 1 for axis in range(values.ndim)]) for axis_at in (source, target)]
    chosen = jax.random.permutation(rng, shards_of)[partner]
    strong = (owner == chosen) | (owner == (partner + shards_of // 2) % shards_of)
    return jnp.where(strong, factor * values, values)


def steps_of(stream_key, dims, cuts, low, top_value):
    def one(axis_at, shards_of):
        draws = jax.random.uniform(jax.random.fold_in(jax.random.fold_in(stream_key, 6), axis_at), (shards_of,), jnp.float32, low / len(cuts), top_value / len(cuts))
        return jnp.repeat(jnp.exp(draws), dims[axis_at] // shards_of).reshape((-1,) + (1,) * (len(dims) - axis_at - 1))

    gain = one(*cuts[0])
    for cut in cuts[1:]:
        gain = gain * one(*cut)
    return gain


def bell_draw(own_key, dims, spread, most, shards=(), kind=jnp.bfloat16):
    level = steps_of(own_key, dims, shards, -0.22, 0.18) if shards else 1.0
    array = jax.random.normal(own_key, dims, jnp.float32) * spread * level
    return jnp.minimum(jnp.maximum(array, -most), most).astype(kind)


def gaussian_with(key, extent, width, reach, cuts, heavy, kind=jnp.bfloat16):
    array = width * jax.random.normal(key, extent, jnp.float32)
    if cuts:
        array = array * steps_of(key, extent, cuts, -0.22, 0.18)
    return jnp.clip(with_spikes(array, jax.random.fold_in(key, 3), *heavy), -reach, reach).astype(kind)


def setup_inputs(seed: int = 0) -> dict:
    key_of = jax.random.split(jax.random.key(seed), 9)
    return {
        "load": bell_draw(key_of[0], (GRID_R, GRID_C, NI, R), 1.0, 6.0, ((0, 16), (1, 16)), jnp.float32),
        "guess": bell_draw(key_of[1], (GRID_R, GRID_C, NI, R), 1.0, 6.0, ((0, 16), (1, 16)), jnp.float32),
        "interface_op": draw_interface_op(jax.random.fold_in(key_of[8], 71), 0),
        "precond": draw_precond(jax.random.fold_in(key_of[8], 71), 0),
        "basis": bell_draw(key_of[4], (GRID_R, GRID_C, NI, NB), (NI // 4) ** -0.5, 0.375, ((0, 16), (1, 16))),
        "coarse_inverse": gaussian_with(key_of[5], (COARSE, COARSE), COARSE ** -0.5, 0.0625, ((0, 16), (1, 16)), (1, 0, 16, 2.0)),
        "edge_rows": jax.vmap(lambda own: jax.random.permutation(own, NI))(jax.random.split(key_of[6], GRID_R * GRID_C)).reshape((GRID_R, GRID_C, NI)).astype(jnp.int32),
        "coarse_slot": jax.vmap(lambda own: jax.random.permutation(own, NB))(jax.random.split(key_of[7], GRID_R * GRID_C)).reshape((GRID_R, GRID_C, NB)).astype(jnp.int32),
    }


OMEGA = 0.6


def local_apply(mats, vecs):
    flat_mats = mats.reshape((GRID_R * GRID_C,) + mats.shape[2:])
    flat_vecs = vecs.reshape((GRID_R * GRID_C,) + vecs.shape[2:])
    result = lax.map(lambda pair: jnp.dot(pair[0], pair[1], preferred_element_type=jnp.float32), (flat_mats, flat_vecs))
    return result.reshape((GRID_R, GRID_C) + result.shape[1:])


def edge_values(field, edge_rows):
    picked = jnp.take_along_axis(field, edge_rows[..., None], axis=2)
    return picked.reshape(GRID_R, GRID_C, 4, NI // 4, R)


def neighbour_values(edges):
    zero_col = jnp.zeros_like(edges[:, :1, 0])
    west = jnp.concatenate([zero_col, edges[:, :-1, 1]], axis=1)
    east = jnp.concatenate([edges[:, 1:, 0], zero_col], axis=1)
    zero_row = jnp.zeros_like(edges[:1, :, 0])
    south = jnp.concatenate([zero_row, edges[:-1, :, 3]], axis=0)
    north = jnp.concatenate([edges[1:, :, 2], zero_row], axis=0)
    return jnp.stack([west, east, south, north], axis=2)


def place(values, inverse):
    flat = values.reshape(GRID_R, GRID_C, NI, R)
    return jnp.take_along_axis(flat, inverse[..., None], axis=2)


def reference(load, guess, interface_op, precond, basis, coarse_inverse, edge_rows, coarse_slot):
    inverse = jnp.argsort(edge_rows, axis=2).astype(jnp.int32)
    slot_inverse = jnp.argsort(coarse_slot, axis=2).astype(jnp.int32)
    grid_row = jnp.arange(GRID_R, dtype=jnp.int32)[:, None] + jnp.zeros((GRID_R, GRID_C), jnp.int32)
    grid_col = jnp.arange(GRID_C, dtype=jnp.int32)[None, :] + jnp.zeros((GRID_R, GRID_C), jnp.int32)
    present = jnp.stack([grid_col > 0, grid_col < GRID_C - 1, grid_row > 0, grid_row < GRID_R - 1], axis=2)
    present = present.astype(jnp.float32)[..., None, None]
    basis_t = jnp.swapaxes(basis, 2, 3)
    current = guess
    for sweep in range(ITERS):
        applied = local_apply(interface_op, current.astype(jnp.bfloat16))
        resid = load - applied - place(neighbour_values(edge_values(applied, edge_rows)), inverse)
        resid_bf = resid.astype(jnp.bfloat16)
        local_fix = local_apply(precond, resid_bf)
        own = edge_values(local_fix, edge_rows)
        smooth_fix = local_fix + 0.5 * place(present * (neighbour_values(own) - own), inverse)
        coarse_res = local_apply(basis_t, resid_bf).astype(jnp.bfloat16)
        coarse_vec = jnp.take_along_axis(coarse_res, slot_inverse[..., None], axis=2).reshape(COARSE, R)
        coarse_sol = jnp.dot(coarse_inverse, coarse_vec, preferred_element_type=jnp.float32).astype(jnp.bfloat16)
        coarse_sol = coarse_sol.reshape(GRID_R, GRID_C, NB, R)
        picked = jnp.take_along_axis(coarse_sol, coarse_slot[..., None], axis=2)
        coarse_fix = local_apply(basis, picked)
        current = current + OMEGA * (smooth_fix + coarse_fix)
    return current
```

```python
import jax
import jax.numpy as jnp
from jax import lax
from jax.experimental import pallas as pl
from jax.experimental.pallas import tpu as pltpu
from jax.sharding import PartitionSpec as P

ITERS = 2
OMEGA = 0.6
MESH = pl.DeviceIdType.MESH
BF = jnp.bfloat16
F32 = jnp.float32
TILE = 256


def mm(left, right):
    return jnp.dot(left, right, preferred_element_type=F32)


def mm_nt(left, right):
    return lax.dot_general(left, right, (((1,), (1,)), ((), ())), preferred_element_type=F32)


def kernel(
    load_h, guess_h, op_h, pre_h, basis_h, coarse_h, rows_h, slot_h, out_h,
    u, load, amat, mmat, cmat, basis, rows, slot,
    pick, place, b2, b2t, keep, ub, applied, resid, fix,
    esend, erecv, cres, gath, ypart, yown, xrecv, zpart, zown, zrecv,
    in_sem, out_sem, e_ss, e_rs, t_ss, t_rs, y_ss, y_rs, p_ss, p_rs, x_ss, x_rs, z_ss, z_rs,
):
    core = lax.axis_index("grp")
    row = lax.axis_index("row")
    col = lax.axis_index("col")
    y, zl = row // 2, lax.rem(row, 2)
    x, zh = col // 4, lax.rem(col, 4)
    a = core * 8 + row
    n_basis = basis.shape[1]

    def at_row(r, c):
        return {"grp": r // 8, "row": lax.rem(r, 8), "col": c}

    loads = [
        pltpu.make_async_copy(src, dst, in_sem.at[i])
        for i, (src, dst) in enumerate(
            [
                (rows_h.at[0], rows),
                (guess_h.at[0, 0], u),
                (op_h.at[0, 0], amat),
                (load_h.at[0, 0], load),
                (slot_h.at[0], slot),
                (basis_h.at[0, 0], basis),
                (pre_h.at[0, 0], mmat),
                (coarse_h, cmat),
            ]
        )
    ]
    for c in loads:
        c.start()
    l_rows, l_u, l_a, l_load, l_slot, l_basis, l_m, l_c = loads

    present = [col > 0, col < 15, a > 0, a < 15]
    across = [at_row(a, col - 1), at_row(a, col + 1), at_row(a - 1, col), at_row(a + 1, col)]
    off_diag = a != col
    mirror = at_row(col, a)
    y_peer = [{"grp": core, "row": lax.rem(y + d, 4) * 2 + zl, "col": col} for d in (1, 2, 3)]
    z_pair = {"grp": core, "row": y * 2 + 1 - zl, "col": col}
    c_pair = {"grp": 1 - core, "row": row, "col": col}
    x_peer = [{"grp": core, "row": row, "col": lax.rem(x + d, 4) * 4 + zh} for d in (1, 2, 3)]
    h_peer = [{"grp": core, "row": row, "col": x * 4 + lax.rem(zh + d, 4)} for d in (1, 2, 3)]

    barrier = pltpu.get_barrier_semaphore()
    fixed = y_peer + [z_pair, c_pair] + x_peer + h_peer
    for peer in fixed:
        pl.semaphore_signal(barrier, inc=1, device_id=peer, device_id_type=MESH)
    for ok, peer in zip(present + [off_diag], across + [mirror]):
        @pl.when(ok)
        def _():
            pl.semaphore_signal(barrier, inc=1, device_id=peer, device_id_type=MESH)

    for k in range(4):
        @pl.when(jnp.logical_not(present[k]))
        def _():
            for e in range(2 * ITERS):
                erecv[e, k] = jnp.zeros(erecv.shape[2:], BF)

    l_rows.wait()
    ni = pick.shape[0]

    @pl.loop(0, ni // 128)
    def _(t):
        base = pl.multiple_of(t * 128, 128)
        here = rows[:, pl.ds(base, 128)].astype(F32)
        down = jnp.broadcast_to(here, (128, 128)).T.astype(jnp.int32)
        lane = lax.broadcasted_iota(jnp.int32, (128, 128), 1)
        for v in range(ni // 128):
            pick[pl.ds(base, 128), v * 128:(v + 1) * 128] = jnp.where(
                down == lane + v * 128, 1.0, 0.0
            ).astype(BF)
        sub = lax.broadcasted_iota(jnp.int32, (128, ni), 0) + base
        place[pl.ds(base, 128), :] = jnp.where(sub == rows[...], 1.0, 0.0).astype(BF)

    def tiles(body):
        @pl.loop(0, ni // TILE)
        def _(t):
            body(pl.ds(pl.multiple_of(t * TILE, TILE), TILE))

    flag = jnp.concatenate(
        [jnp.full((TILE, 128), p.astype(F32)) for p in present], axis=0
    ).astype(BF)

    def keep_tile(at):
        keep[at, :] = 1.0 - 0.5 * mm(place[at, :], flag)

    tiles(keep_tile)

    l_u.wait()
    ub[...] = u[...].astype(BF)

    l_slot.wait()
    l_basis.wait()
    order = (lax.broadcasted_iota(jnp.int32, (n_basis, n_basis), 0) == slot[...])
    order = jnp.where(order, 1.0, 0.0).astype(BF)
    b2t[...] = mm_nt(order, basis[...]).astype(BF)
    b2[...] = mm_nt(basis[...], order).astype(BF)

    l_a.wait()

    total = 11 + sum(p.astype(jnp.int32) for p in present) + off_diag.astype(jnp.int32)
    pl.semaphore_wait(barrier, total)

    def edge_copy(e, k):
        return pltpu.make_async_remote_copy(
            src_ref=esend.at[e, k], dst_ref=erecv.at[e, k ^ 1],
            send_sem=e_ss.at[e, k], recv_sem=e_rs.at[e, k ^ 1],
            device_id=across[k], device_id_type=MESH,
        )

    def edge_arrival(e, k):
        return pltpu.make_async_remote_copy(
            src_ref=esend.at[e, k], dst_ref=erecv.at[e, k],
            send_sem=e_ss.at[e, k], recv_sem=e_rs.at[e, k],
            device_id=across[k], device_id_type=MESH,
        )

    def send_edges(e, source):
        for k in (0, 1, 2, 3):
            esend[e, k] = mm(pick[k * TILE:(k + 1) * TILE, :], source).astype(BF)

            @pl.when(present[k])
            def _():
                edge_copy(e, k).start()

    def take_edges(e):
        for k in range(4):
            @pl.when(present[k])
            def _():
                edge_arrival(e, k).wait_recv()

    def beside(e):
        return erecv[e].reshape(ni, erecv.shape[3])

    for s in range(ITERS):
        e1, e2 = 2 * s, 2 * s + 1

        def apply_tile(at):
            value = mm(amat[at, :], ub[...])
            applied[at, :] = value
            resid[at, :] = value.astype(BF)

        tiles(apply_tile)
        send_edges(e1, resid[...])
        if s == 0:
            l_load.wait()
        take_edges(e1)

        def resid_tile(at):
            value = load[at, :] - applied[at, :] - mm(place[at, :], beside(e1))
            resid[at, :] = value.astype(BF)

        tiles(resid_tile)

        cres[s] = mm(b2t[...], resid[...]).astype(BF)
        crossing = pltpu.make_async_remote_copy(
            src_ref=cres.at[s],
            dst_ref=gath.at[s, col // 8, lax.rem(col, 8) // 2, lax.rem(col, 2)],
            send_sem=t_ss.at[s], recv_sem=t_rs.at[s],
            device_id=mirror, device_id_type=MESH,
        )

        @pl.when(off_diag)
        def _():
            crossing.start()

        @pl.when(jnp.logical_not(off_diag))
        def _():
            gath[s, core, y, zl] = cres[s]

        if s == 0:
            l_m.wait()

        def fix_tile(at):
            value = mm(mmat[at, :], resid[...])
            fix[at, :] = value
            applied[at, :] = value

        tiles(fix_tile)

        @pl.when(off_diag)
        def _():
            crossing.wait_recv()

        mine = gath.at[s, core, y, zl]
        y_copies = [
            pltpu.make_async_remote_copy(
                src_ref=mine, dst_ref=mine,
                send_sem=y_ss.at[s, d], recv_sem=y_rs.at[s, d],
                device_id=y_peer[d], device_id_type=MESH,
            )
            for d in range(3)
        ]
        for c in y_copies:
            c.start()
        for c in y_copies:
            c.wait_recv()
        group = gath.at[s, core, :, zl]
        others = gath.at[s, core, :, 1 - zl]

        def pair_copy(i, ref, peer):
            return pltpu.make_async_remote_copy(
                src_ref=ref, dst_ref=ref,
                send_sem=p_ss.at[s, i], recv_sem=p_rs.at[s, i],
                device_id=peer, device_id_type=MESH,
            )

        z_copy = pair_copy(0, group, z_pair)
        c_copy = pair_copy(1, group, c_pair)
        o_copy = pair_copy(2, others, c_pair)
        z_copy.start()
        c_copy.start()

        ub[...] = fix[...].astype(BF)
        send_edges(e2, ub[...])

        z_copy.wait_recv()
        o_copy.start()
        c_copy.wait_recv()
        o_copy.wait_recv()
        if s == 0:
            l_c.wait()
        vec = gath[s].reshape(ni, gath.shape[5])

        x_copies = []
        for d in (2, 1, 3, 0):
            to = lax.rem(x + d, 4)
            block = mm(cmat[pl.ds(pl.multiple_of(to * TILE, TILE), TILE), :], vec)
            if d == 0:
                yown[...] = block
            else:
                ypart[s, d - 1] = block.astype(BF)
                c = pltpu.make_async_remote_copy(
                    src_ref=ypart.at[s, d - 1], dst_ref=xrecv.at[s, d - 1],
                    send_sem=x_ss.at[s, d - 1], recv_sem=x_rs.at[s, d - 1],
                    device_id=x_peer[d - 1], device_id_type=MESH,
                )
                c.start()
                x_copies.append(c)
        for c in x_copies:
            c.wait_recv()
        total_x = yown[...]
        for d in range(3):
            total_x = total_x + xrecv[s, d].astype(F32)
        total_x = total_x.reshape(zown.shape)
        zown[...] = total_x
        zpart[s] = total_x.astype(BF)
        h_copies = [
            pltpu.make_async_remote_copy(
                src_ref=zpart.at[s, lax.rem(zh + d + 1, 4)], dst_ref=zrecv.at[s, d],
                send_sem=z_ss.at[s, d], recv_sem=z_rs.at[s, d],
                device_id=h_peer[d], device_id_type=MESH,
            )
            for d in range(3)
        ]
        for c in h_copies:
            c.start()
        take_edges(e2)

        def smooth_tile(at):
            weight = jnp.concatenate([keep[at, :]] * 2, axis=1)
            fix[at, :] = weight * fix[at, :] + 0.5 * mm(place[at, :], beside(e2))

        tiles(smooth_tile)
        for c in h_copies:
            c.wait_recv()
        sol = zown[zh]
        for d in range(3):
            sol = sol + zrecv[s, d].astype(F32)
        sol = sol.astype(BF)

        def update_tile(at):
            value = u[at, :] + OMEGA * (fix[at, :] + mm(b2[at, :], sol))
            u[at, :] = value
            ub[at, :] = value.astype(BF)

        tiles(update_tile)

        @pl.when(off_diag)
        def _():
            crossing.wait_send()
        for c in y_copies + [z_copy, c_copy, o_copy] + x_copies + h_copies:
            c.wait_send()
        for e in (e1, e2):
            for k in range(4):
                @pl.when(present[k])
                def _():
                    edge_copy(e, k).wait_send()

    done = pltpu.make_async_copy(u, out_h.at[0, 0], out_sem)
    done.start()
    done.wait()


def body(load, guess, interface_op, precond, basis, coarse_inverse, edge_rows, coarse_slot):
    ni, cases = load.shape[2:]
    nb = basis.shape[3]
    dma = pltpu.SemaphoreType.DMA
    vm = pltpu.VMEM
    anywhere = pl.BlockSpec(memory_space=pl.ANY)
    return pl.pallas_call(
        kernel,
        out_shape=jax.ShapeDtypeStruct(load.shape, F32),
        in_specs=[anywhere] * 8,
        out_specs=anywhere,
        scratch_shapes=[
            vm((ni, cases), F32), vm((ni, cases), F32),
            vm((ni, ni), BF), vm((ni, ni), BF), vm((ni, ni), BF),
            vm((ni, nb), BF), vm((1, ni), jnp.int32), vm((1, nb), jnp.int32),
            vm((ni, ni), BF), vm((ni, ni), BF), vm((ni, nb), BF), vm((nb, ni), BF),
            vm((ni, 128), F32), vm((ni, cases), BF), vm((ni, cases), F32),
            vm((ni, cases), BF), vm((ni, cases), F32),
            vm((2 * ITERS, 4, ni // 4, cases), BF), vm((2 * ITERS, 4, ni // 4, cases), BF),
            vm((ITERS, nb, cases), BF), vm((ITERS, 2, 4, 2, nb, cases), BF),
            vm((ITERS, 3, TILE, cases), BF), vm((TILE, cases), F32),
            vm((ITERS, 3, TILE, cases), BF),
            vm((ITERS, 4, nb, cases), BF), vm((4, nb, cases), F32), vm((ITERS, 3, nb, cases), BF),
            dma((8,)), dma,
            dma((2 * ITERS, 4)), dma((2 * ITERS, 4)),
            dma((ITERS,)), dma((ITERS,)),
            dma((ITERS, 3)), dma((ITERS, 3)),
            dma((ITERS, 3)), dma((ITERS, 3)),
            dma((ITERS, 3)), dma((ITERS, 3)),
            dma((ITERS, 3)), dma((ITERS, 3)),
        ],
        compiler_params=pltpu.CompilerParams(
            collective_id=0, has_side_effects=True, vmem_limit_bytes=48 * 1024 * 1024
        ),
    )(load, guess, interface_op, precond, basis, coarse_inverse, edge_rows, coarse_slot)


def solution(mesh):
    cells = (("grp", "row"), "col")
    return jax.shard_map(
        body,
        mesh=mesh,
        in_specs=(
            P(*cells, None, None),
            P(*cells, None, None),
            P(*cells, None, None),
            P(*cells, None, None),
            P(*cells, None, None),
            P(*cells),
            P(*cells, None),
            P(*cells, None),
        ),
        out_specs=P(*cells, None, None),
        check_vma=False,
    )
```

```python
import jax
import jax.numpy as jnp
from jax import lax
from jax.experimental import pallas as pl
from jax.experimental.pallas import tpu as pltpu
from jax.sharding import PartitionSpec as P

ITERS = 2
OMEGA = 0.6
MESH = pl.DeviceIdType.MESH
BF = jnp.bfloat16
F32 = jnp.float32
TILE = 256


def mm(left, right):
    return jnp.dot(left, right, preferred_element_type=F32)


def kernel(
    load_h, guess_h, op_h, pre_h, basis_h, coarse_h, rows_h, slot_h, out_h,
    u, load, amat, mmat, cmat, basis, rows, slot,
    pick, place, b2, b2t, keep, ub, applied, resid, fix,
    esend, erecv, cres, gath, ypart, yown, xrecv, zpart, zrecv,
    in_sem, out_sem, e_ss, e_rs, t_ss, t_rs, y_ss, y_rs, p_ss, p_rs, x_ss, x_rs, z_ss, z_rs,
):
    core = lax.axis_index("grp")
    row = lax.axis_index("row")
    col = lax.axis_index("col")
    y, zl = row // 2, lax.rem(row, 2)
    x, zh = col // 4, lax.rem(col, 4)
    a = core * 8 + row
    n_basis = basis.shape[0]

    def at_row(r, c):
        return {"grp": r // 8, "row": lax.rem(r, 8), "col": c}

    loads = [
        pltpu.make_async_copy(src, dst, in_sem.at[i])
        for i, (src, dst) in enumerate(
            [
                (rows_h.at[0], rows),
                (guess_h.at[0, 0], u),
                (op_h.at[0, 0], amat),
                (load_h.at[0, 0], load),
                (slot_h.at[0], slot),
                (basis_h, basis),
                (pre_h.at[0, 0], mmat),
                (coarse_h, cmat),
            ]
        )
    ]
    for c in loads:
        c.start()
    l_rows, l_u, l_a, l_load, l_slot, l_basis, l_m, l_c = loads

    present = [col > 0, col < 15, a > 0, a < 15]
    across = [at_row(a, col - 1), at_row(a, col + 1), at_row(a - 1, col), at_row(a + 1, col)]
    stays = [jnp.logical_and(a == col, zl == j) for j in range(2)]
    mirror = [at_row(col // 2 * 2 + j, a) for j in range(2)]
    y_peer = [{"grp": core, "row": lax.rem(y + d, 4) * 2 + zl, "col": col} for d in (1, 2, 3)]
    c_pair = {"grp": 1 - core, "row": row, "col": col}
    x_peer = [{"grp": core, "row": row, "col": lax.rem(x + d, 4) * 4 + zh} for d in (1, 2, 3)]
    h_peer = [{"grp": core, "row": row, "col": x * 4 + lax.rem(zh + d, 4)} for d in (1, 2, 3)]

    barrier = pltpu.get_barrier_semaphore()
    fixed = y_peer + [c_pair] + x_peer + h_peer
    leaves = [jnp.logical_not(p) for p in stays]
    source = [at_row(col, a // 2 * 2 + j) for j in range(2)]
    for peer in fixed:
        pl.semaphore_signal(barrier, inc=1, device_id=peer, device_id_type=MESH)
    for ok, peer in zip(present + leaves, across + source):
        @pl.when(ok)
        def _():
            pl.semaphore_signal(barrier, inc=1, device_id=peer, device_id_type=MESH)

    for k in range(4):
        @pl.when(jnp.logical_not(present[k]))
        def _():
            for e in range(2 * ITERS):
                erecv[e, k] = jnp.zeros(erecv.shape[2:], BF)

    l_rows.wait()
    ni = pick.shape[0]

    @pl.loop(0, ni // 128)
    def _(t):
        base = pl.multiple_of(t * 128, 128)
        here = rows[:, pl.ds(base, 128)].astype(F32)
        down = jnp.broadcast_to(here, (128, 128)).T.astype(jnp.int32)
        lane = lax.broadcasted_iota(jnp.int32, (128, 128), 1)
        for v in range(ni // 128):
            pick[pl.ds(base, 128), v * 128:(v + 1) * 128] = jnp.where(
                down == lane + v * 128, 1.0, 0.0
            ).astype(BF)
        sub = lax.broadcasted_iota(jnp.int32, (128, ni), 0) + base
        place[pl.ds(base, 128), :] = jnp.where(sub == rows[...], 1.0, 0.0).astype(BF)

    def tiles(body):
        for t in range(ni // TILE):
            body(pl.ds(t * TILE, TILE))

    l_u.wait()
    ub[...] = u[...].astype(BF)

    l_a.wait()

    total = len(fixed) + sum(p.astype(jnp.int32) for p in present + leaves)
    pl.semaphore_wait(barrier, total)

    def edge_copy(e, k):
        return pltpu.make_async_remote_copy(
            src_ref=esend.at[e, k], dst_ref=erecv.at[e, k ^ 1],
            send_sem=e_ss.at[e, k], recv_sem=e_rs.at[e, k ^ 1],
            device_id=across[k], device_id_type=MESH,
        )

    def edge_arrival(e, k):
        return pltpu.make_async_remote_copy(
            src_ref=esend.at[e, k], dst_ref=erecv.at[e, k],
            send_sem=e_ss.at[e, k], recv_sem=e_rs.at[e, k],
            device_id=across[k], device_id_type=MESH,
        )

    def send_edges(e, source):
        for k in (0, 1, 2, 3):
            esend[e, k] = mm(pick[k * TILE:(k + 1) * TILE, :], source).astype(BF)

            @pl.when(present[k])
            def _():
                edge_copy(e, k).start()

    def take_edges(e):
        for k in range(4):
            @pl.when(present[k])
            def _():
                edge_arrival(e, k).wait_recv()

    def beside(e):
        return erecv[e].reshape(ni, erecv.shape[3])

    def prepare():
        flag = jnp.concatenate(
            [jnp.full((TILE, 128), p.astype(F32)) for p in present], axis=0
        ).astype(BF)

        def keep_tile(at):
            keep[at, :] = 1.0 - 0.5 * mm(place[at, :], flag)

        tiles(keep_tile)

        l_slot.wait()
        l_basis.wait()
        order = (lax.broadcasted_iota(jnp.int32, (n_basis, n_basis), 0) == slot[...])
        order = jnp.where(order, 1.0, 0.0).astype(BF)
        ordered = mm(order, basis[...])
        b2t[...] = ordered.astype(BF)
        b2[...] = ordered.T.astype(BF)

    for s in range(ITERS):
        e1, e2 = 2 * s, 2 * s + 1

        def apply_tile(at):
            value = mm(amat[at, :], ub[...])
            applied[at, :] = value
            resid[at, :] = value.astype(BF)

        tiles(apply_tile)
        send_edges(e1, resid[...])
        if s == 0:
            prepare()
            l_load.wait()
        take_edges(e1)

        def resid_tile(at):
            value = load[at, :] - applied[at, :] - mm(place[at, :], beside(e1))
            resid[at, :] = value.astype(BF)

        tiles(resid_tile)

        cres[s] = mm(b2t[...], resid[...]).astype(BF)
        slot_of = gath.at[s, col // 8, lax.rem(col, 8) // 2, lax.rem(col, 2)]
        crossings = [
            pltpu.make_async_remote_copy(
                src_ref=cres.at[s], dst_ref=slot_of,
                send_sem=t_ss.at[s, j], recv_sem=t_rs.at[s, lax.rem(col, 2)],
                device_id=mirror[j], device_id_type=MESH,
            )
            for j in range(2)
        ]
        arrivals = [
            pltpu.make_async_remote_copy(
                src_ref=cres.at[s], dst_ref=gath.at[s, core, y, j],
                send_sem=t_ss.at[s, j], recv_sem=t_rs.at[s, j],
                device_id=source[j], device_id_type=MESH,
            )
            for j in range(2)
        ]
        for j in range(2):
            @pl.when(leaves[j])
            def _():
                crossings[j].start()

            @pl.when(stays[j])
            def _():
                gath[s, core, y, j] = cres[s]

        if s == 0:
            l_m.wait()

        def fix_tile(at):
            value = mm(mmat[at, :], resid[...])
            fix[at, :] = value
            applied[at, :] = value

        tiles(fix_tile)

        for j in range(2):
            @pl.when(leaves[j])
            def _():
                arrivals[j].wait_recv()

        def gather_copy(i, from_y, sems, peer):
            ref = gath.at[s, core, from_y]
            return pltpu.make_async_remote_copy(
                src_ref=ref, dst_ref=ref,
                send_sem=sems[0].at[s, i], recv_sem=sems[1].at[s, i],
                device_id=peer, device_id_type=MESH,
            )

        y_sems, p_sems = (y_ss, y_rs), (p_ss, p_rs)
        y_copies = [gather_copy(d, y, y_sems, y_peer[d]) for d in range(3)]
        for c in y_copies:
            c.start()
        p_copies = [gather_copy(3, y, p_sems, c_pair)]
        p_copies[0].start()

        ub[...] = fix[...].astype(BF)
        send_edges(e2, ub[...])

        for d in (0, 2, 1):
            from_y = lax.rem(y + 3 - d, 4)
            gather_copy(d, from_y, y_sems, y_peer[d]).wait_recv()
            c = gather_copy(d, from_y, p_sems, c_pair)
            c.start()
            p_copies.append(c)
        for d, c in zip((3, 0, 2, 1), p_copies):
            at_y = y if d == 3 else lax.rem(y + 3 - d, 4)
            other = gath.at[s, 1 - core, at_y]
            pltpu.make_async_remote_copy(
                src_ref=other, dst_ref=other,
                send_sem=p_ss.at[s, d], recv_sem=p_rs.at[s, d],
                device_id=c_pair, device_id_type=MESH,
            ).wait_recv()
        if s == 0:
            l_c.wait()
        vec = gath[s].reshape(ni, gath.shape[5])

        def block_of(d):
            to = lax.rem(x + d, 4)
            return mm(cmat[pl.ds(pl.multiple_of(to * TILE, TILE), TILE), :], vec)

        for d in range(3):
            ypart[s, d] = block_of(d + 1).astype(BF).reshape(ypart.shape[2:])

        def x_copy(j, d):
            at_h = lax.rem(zh + (2, 1, 3, 0)[j], 4)
            return pltpu.make_async_remote_copy(
                src_ref=ypart.at[s, d, at_h], dst_ref=xrecv.at[s, d, at_h],
                send_sem=x_ss.at[s, d, j], recv_sem=x_rs.at[s, d, j],
                device_id=x_peer[d], device_id_type=MESH,
            )

        x_copies = [x_copy(j, d) for j in range(4) for d in (1, 0, 2)]
        for c in x_copies:
            c.start()
        yown[...] = block_of(0).reshape(yown.shape)
        h_copies = []
        for j in range(4):
            dz = (2, 1, 3, 0)[j]
            at_h = lax.rem(zh + dz, 4)
            for c in x_copies[3 * j:3 * j + 3]:
                c.wait_recv()
            part = yown[at_h]
            for d in range(3):
                part = part + xrecv[s, d, at_h].astype(F32)
            if dz == 0:
                sol = part
                continue
            zpart[s, dz - 1] = part.astype(BF)
            c = pltpu.make_async_remote_copy(
                src_ref=zpart.at[s, dz - 1], dst_ref=zrecv.at[s, dz - 1],
                send_sem=z_ss.at[s, dz - 1], recv_sem=z_rs.at[s, dz - 1],
                device_id=h_peer[dz - 1], device_id_type=MESH,
            )
            c.start()
            h_copies.append(c)
        take_edges(e2)

        def smooth_tile(at):
            weight = jnp.concatenate([keep[at, :]] * 2, axis=1)
            fix[at, :] = weight * fix[at, :] + 0.5 * mm(place[at, :], beside(e2))

        tiles(smooth_tile)
        for c in h_copies:
            c.wait_recv()
        for d in range(3):
            sol = sol + zrecv[s, d].astype(F32)
        sol = sol.astype(BF)

        def update_tile(at):
            value = u[at, :] + OMEGA * (fix[at, :] + mm(b2[at, :], sol))
            u[at, :] = value
            ub[at, :] = value.astype(BF)

        tiles(update_tile)

        for j in range(2):
            @pl.when(leaves[j])
            def _():
                crossings[j].wait_send()
        for c in y_copies + p_copies + x_copies + h_copies:
            c.wait_send()
        for e in (e1, e2):
            for k in range(4):
                @pl.when(present[k])
                def _():
                    edge_copy(e, k).wait_send()

    done = pltpu.make_async_copy(u, out_h.at[0, 0], out_sem)
    done.start()
    done.wait()


def body(load, guess, interface_op, precond, basis, coarse_inverse, edge_rows, coarse_slot):
    ni, cases = load.shape[2:]
    nb = basis.shape[3]
    dma = pltpu.SemaphoreType.DMA
    vm = pltpu.VMEM
    anywhere = pl.BlockSpec(memory_space=pltpu.HBM)
    return pl.pallas_call(
        kernel,
        out_shape=jax.ShapeDtypeStruct(load.shape, F32),
        in_specs=[anywhere] * 8,
        out_specs=anywhere,
        scratch_shapes=[
            vm((ni, cases), F32), vm((ni, cases), F32),
            vm((ni, ni), BF), vm((ni, ni), BF), vm((ni, ni), BF),
            vm((nb, ni), BF), vm((1, ni), jnp.int32), vm((1, nb), jnp.int32),
            vm((ni, ni), BF), vm((ni, ni), BF), vm((ni, nb), BF), vm((nb, ni), BF),
            vm((ni, 128), F32), vm((ni, cases), BF), vm((ni, cases), F32),
            vm((ni, cases), BF), vm((ni, cases), F32),
            vm((2 * ITERS, 4, ni // 4, cases), BF), vm((2 * ITERS, 4, ni // 4, cases), BF),
            vm((ITERS, nb, cases), BF), vm((ITERS, 2, 4, 2, nb, cases), BF),
            vm((ITERS, 3, 4, nb, cases), BF), vm((4, nb, cases), F32),
            vm((ITERS, 3, 4, nb, cases), BF),
            vm((ITERS, 3, nb, cases), BF), vm((ITERS, 3, nb, cases), BF),
            dma((8,)), dma,
            dma((2 * ITERS, 4)), dma((2 * ITERS, 4)),
            dma((ITERS, 2)), dma((ITERS, 2)),
            dma((ITERS, 3)), dma((ITERS, 3)),
            dma((ITERS, 4)), dma((ITERS, 4)),
            dma((ITERS, 3, 4)), dma((ITERS, 3, 4)),
            dma((ITERS, 3)), dma((ITERS, 3)),
        ],
        compiler_params=pltpu.CompilerParams(
            collective_id=0, has_side_effects=True, vmem_limit_bytes=60 * 1024 * 1024
        ),
    )(load, guess, interface_op, precond, basis[0, 0].T, coarse_inverse, edge_rows, coarse_slot)


def solution(mesh):
    cells = (("grp", "row"), "col")
    return jax.shard_map(
        body,
        mesh=mesh,
        in_specs=(
            P(*cells, None, None),
            P(*cells, None, None),
            P(*cells, None, None),
            P(*cells, None, None),
            P(*cells, None, None),
            P(*cells),
            P(*cells, None),
            P(*cells, None),
        ),
        out_specs=P(*cells, None, None),
        check_vma=False,
    )
```

```python
import jax
import jax.numpy as jnp
from jax import lax
from jax.experimental import pallas as pl
from jax.experimental.pallas import tpu as pltpu
from jax.sharding import PartitionSpec as P

ITERS = 2
OMEGA = 0.6
MESH = pl.DeviceIdType.MESH
BF = jnp.bfloat16
F32 = jnp.float32
TILE = 256


def mm(left, right):
    return jnp.dot(left, right, preferred_element_type=F32)


def kernel(
    load_h, guess_h, op_h, pre_h, basis_h, coarse_h, rows_h, slot_h, out_h,
    u, load, amat, mmat, cmat, basis, rows, slot,
    pick, place, b2, b2t, keep, ub, applied, resid, fix,
    esend, erecv, bedge, bnear, csend, crecv, cres, gath, ypart, yown, xrecv, zpart, zrecv,
    in_sem, out_sem, e_ss, e_rs, n_ss, n_rs, q_ss, q_rs, t_ss, t_rs, y_ss, y_rs, p_ss, p_rs, x_ss, x_rs, z_ss, z_rs,
):
    core = lax.axis_index("grp")
    row = lax.axis_index("row")
    col = lax.axis_index("col")
    y, zl = row // 2, lax.rem(row, 2)
    x, zh = col // 4, lax.rem(col, 4)
    a = core * 8 + row
    n_basis = basis.shape[0]

    def at_row(r, c):
        return {"grp": r // 8, "row": lax.rem(r, 8), "col": c}

    loads = [
        pltpu.make_async_copy(src, dst, in_sem.at[i])
        for i, (src, dst) in enumerate(
            [
                (rows_h.at[0], rows),
                (slot_h.at[0], slot),
                (basis_h, basis),
                (guess_h.at[0, 0], u),
                (op_h.at[0, 0], amat),
                (load_h.at[0, 0], load),
                (pre_h.at[0, 0], mmat),
                (coarse_h, cmat),
            ]
        )
    ]
    for c in loads:
        c.start()
    l_rows, l_slot, l_basis, l_u, l_a, l_load, l_m, l_c = loads

    present = [col > 0, col < 15, a > 0, a < 15]
    across = [at_row(a, col - 1), at_row(a, col + 1), at_row(a - 1, col), at_row(a + 1, col)]
    stays = [jnp.logical_and(a == col, zl == j) for j in range(2)]
    mirror = [at_row(col // 2 * 2 + j, a) for j in range(2)]
    y_peer = [{"grp": core, "row": lax.rem(y + d, 4) * 2 + zl, "col": col} for d in (1, 2, 3)]
    c_pair = {"grp": 1 - core, "row": row, "col": col}
    x_peer = [{"grp": core, "row": row, "col": lax.rem(x + d, 4) * 4 + zh} for d in (1, 2, 3)]
    h_peer = [{"grp": core, "row": row, "col": x * 4 + lax.rem(zh + d, 4)} for d in (1, 2, 3)]

    barrier = pltpu.get_barrier_semaphore()
    fixed = y_peer + [c_pair] + x_peer + h_peer
    leaves = [jnp.logical_not(p) for p in stays]
    source = [at_row(col, a // 2 * 2 + j) for j in range(2)]
    for peer in fixed:
        pl.semaphore_signal(barrier, inc=1, device_id=peer, device_id_type=MESH)
    for ok, peer in zip(present + leaves, across + source):
        @pl.when(ok)
        def _():
            pl.semaphore_signal(barrier, inc=1, device_id=peer, device_id_type=MESH)

    for k in range(4):
        @pl.when(jnp.logical_not(present[k]))
        def _():
            for e in range(2 * ITERS):
                erecv[e, k] = jnp.zeros(erecv.shape[2:], BF)
            for s in range(ITERS):
                crecv[s, k] = jnp.zeros(crecv.shape[2:], BF)

    l_rows.wait()
    ni = pick.shape[0]

    @pl.loop(0, ni // 128)
    def _(t):
        base = pl.multiple_of(t * 128, 128)
        here = rows[:, pl.ds(base, 128)].astype(F32)
        down = jnp.broadcast_to(here, (128, 128)).T.astype(jnp.int32)
        lane = lax.broadcasted_iota(jnp.int32, (128, 128), 1)
        for v in range(ni // 128):
            pick[pl.ds(base, 128), v * 128:(v + 1) * 128] = jnp.where(
                down == lane + v * 128, 1.0, 0.0
            ).astype(BF)
        sub = lax.broadcasted_iota(jnp.int32, (128, ni), 0) + base
        place[pl.ds(base, 128), :] = jnp.where(sub == rows[...], 1.0, 0.0).astype(BF)

    def tiles(body):
        for t in range(ni // TILE):
            body(pl.ds(t * TILE, TILE))

    l_slot.wait()
    l_basis.wait()
    order = (lax.broadcasted_iota(jnp.int32, (n_basis, n_basis), 0) == slot[...])
    order = jnp.where(order, 1.0, 0.0).astype(BF)
    ordered = mm(order, basis[...])
    b2t[...] = ordered.astype(BF)
    b2[...] = ordered.T.astype(BF)
    for k in range(4):
        bedge[k] = mm(b2t[...], place[:, k * TILE:(k + 1) * TILE]).astype(BF)


    total = len(fixed) + sum(p.astype(jnp.int32) for p in present + leaves)
    pl.semaphore_wait(barrier, total)

    def edge_copy(e, k):
        return pltpu.make_async_remote_copy(
            src_ref=esend.at[e, k], dst_ref=erecv.at[e, k ^ 1],
            send_sem=e_ss.at[e, k], recv_sem=e_rs.at[e, k ^ 1],
            device_id=across[k], device_id_type=MESH,
        )

    def edge_arrival(e, k):
        return pltpu.make_async_remote_copy(
            src_ref=esend.at[e, k], dst_ref=erecv.at[e, k],
            send_sem=e_ss.at[e, k], recv_sem=e_rs.at[e, k],
            device_id=across[k], device_id_type=MESH,
        )

    def select_edge(e, k, source):
        esend[e, k] = mm(pick[k * TILE:(k + 1) * TILE, :], source).astype(BF)

    def start_edge(e, k):
        @pl.when(present[k])
        def _():
            edge_copy(e, k).start()

    def basis_copy(k, to):
        return pltpu.make_async_remote_copy(
            src_ref=bedge.at[k], dst_ref=bnear.at[to],
            send_sem=n_ss.at[k], recv_sem=n_rs.at[to],
            device_id=across[k], device_id_type=MESH,
        )

    def product_copy(s, k, to):
        return pltpu.make_async_remote_copy(
            src_ref=csend.at[s, k], dst_ref=crecv.at[s, to],
            send_sem=q_ss.at[s, k], recv_sem=q_rs.at[s, to],
            device_id=across[k], device_id_type=MESH,
        )

    def take_edges(e):
        for k in range(4):
            @pl.when(present[k])
            def _():
                edge_arrival(e, k).wait_recv()

    def beside(e):
        return erecv[e].reshape(ni, erecv.shape[3])

    def prepare():
        flag = jnp.concatenate(
            [jnp.full((TILE, 128), p.astype(F32)) for p in present], axis=0
        ).astype(BF)

        def keep_tile(at):
            keep[at, :] = 1.0 - 0.5 * mm(place[at, :], flag)

        tiles(keep_tile)

    for k in range(4):
        @pl.when(present[k])
        def _():
            basis_copy(k, k ^ 1).start()

    l_u.wait()
    ub[...] = u[...].astype(BF)
    l_a.wait()

    for s in range(ITERS):
        e1, e2 = 2 * s, 2 * s + 1

        def apply_tile(at):
            value = mm(amat[at, :], ub[...])
            applied[at, :] = value
            resid[at, :] = value.astype(BF)

        tiles(apply_tile)
        for k in range(4):
            select_edge(e1, k, resid[...])
        if s == 0:
            prepare()
        for k in range(4):
            @pl.when(present[k])
            def _():
                if s == 0:
                    basis_copy(k, k).wait_recv()
                csend[s, k] = mm(bnear[k], esend[e1, k]).astype(BF)
                product_copy(s, k, k ^ 1).start()
        for k in range(4):
            start_edge(e1, k)
        if s == 0:
            l_load.wait()

        def own_tile(at):
            resid[at, :] = (load[at, :] - applied[at, :]).astype(BF)

        tiles(own_tile)

        part = mm(b2t[...], resid[...])
        for k in range(4):
            @pl.when(present[k])
            def _():
                product_copy(s, k, k).wait_recv()
        for k in range(4):
            part = part - crecv[s, k].astype(F32)
        cres[s] = part.astype(BF)
        slot_of = gath.at[s, col // 8, lax.rem(col, 8) // 2, lax.rem(col, 2)]
        crossings = [
            pltpu.make_async_remote_copy(
                src_ref=cres.at[s], dst_ref=slot_of,
                send_sem=t_ss.at[s, j], recv_sem=t_rs.at[s, lax.rem(col, 2)],
                device_id=mirror[j], device_id_type=MESH,
            )
            for j in range(2)
        ]
        arrivals = [
            pltpu.make_async_remote_copy(
                src_ref=cres.at[s], dst_ref=gath.at[s, core, y, j],
                send_sem=t_ss.at[s, j], recv_sem=t_rs.at[s, j],
                device_id=source[j], device_id_type=MESH,
            )
            for j in range(2)
        ]
        for j in range(2):
            @pl.when(leaves[j])
            def _():
                crossings[j].start()

            @pl.when(stays[j])
            def _():
                gath[s, core, y, j] = cres[s]

        for j in range(2):
            @pl.when(leaves[j])
            def _():
                arrivals[j].wait_recv()

        def gather_copy(i, from_y, sems, peer):
            ref = gath.at[s, core, from_y]
            return pltpu.make_async_remote_copy(
                src_ref=ref, dst_ref=ref,
                send_sem=sems[0].at[s, i], recv_sem=sems[1].at[s, i],
                device_id=peer, device_id_type=MESH,
            )

        y_sems, p_sems = (y_ss, y_rs), (p_ss, p_rs)
        y_copies = [gather_copy(d, y, y_sems, y_peer[d]) for d in range(3)]
        for c in y_copies:
            c.start()
        p_copies = [gather_copy(3, y, p_sems, c_pair)]
        p_copies[0].start()

        for d in (0, 2, 1):
            from_y = lax.rem(y + 3 - d, 4)
            gather_copy(d, from_y, y_sems, y_peer[d]).wait_recv()
            c = gather_copy(d, from_y, p_sems, c_pair)
            c.start()
            p_copies.append(c)

        take_edges(e1)

        def resid_tile(at):
            value = load[at, :] - applied[at, :] - mm(place[at, :], beside(e1))
            resid[at, :] = value.astype(BF)

        tiles(resid_tile)
        if s == 0:
            l_m.wait()

        def fix_tile(at):
            value = mm(mmat[at, :], resid[...])
            fix[at, :] = value
            ub[at, :] = value.astype(BF)

        tiles(fix_tile)
        for k in range(4):
            select_edge(e2, k, ub[...])
            start_edge(e2, k)

        for d in (3, 0, 2, 1):
            at_y = y if d == 3 else lax.rem(y + 3 - d, 4)
            other = gath.at[s, 1 - core, at_y]
            pltpu.make_async_remote_copy(
                src_ref=other, dst_ref=other,
                send_sem=p_ss.at[s, d], recv_sem=p_rs.at[s, d],
                device_id=c_pair, device_id_type=MESH,
            ).wait_recv()
        if s == 0:
            l_c.wait()
        vec = gath[s].reshape(ni, gath.shape[5])

        def block_of(d):
            to = lax.rem(x + d, 4)
            return mm(cmat[pl.ds(pl.multiple_of(to * TILE, TILE), TILE), :], vec)

        for d in range(3):
            ypart[s, d] = block_of(d + 1).astype(BF).reshape(ypart.shape[2:])

        def x_copy(j, d):
            at_h = lax.rem(zh + (2, 1, 3, 0)[j], 4)
            return pltpu.make_async_remote_copy(
                src_ref=ypart.at[s, d, at_h], dst_ref=xrecv.at[s, d, at_h],
                send_sem=x_ss.at[s, d, j], recv_sem=x_rs.at[s, d, j],
                device_id=x_peer[d], device_id_type=MESH,
            )

        x_copies = [x_copy(j, d) for j in range(4) for d in (1, 0, 2)]
        for c in x_copies:
            c.start()
        yown[...] = block_of(0).reshape(yown.shape)
        h_copies = []
        for j in range(4):
            dz = (2, 1, 3, 0)[j]
            at_h = lax.rem(zh + dz, 4)
            for c in x_copies[3 * j:3 * j + 3]:
                c.wait_recv()
            part = yown[at_h]
            for d in range(3):
                part = part + xrecv[s, d, at_h].astype(F32)
            if dz == 0:
                sol = part
                continue
            zpart[s, dz - 1] = part.astype(BF)
            c = pltpu.make_async_remote_copy(
                src_ref=zpart.at[s, dz - 1], dst_ref=zrecv.at[s, dz - 1],
                send_sem=z_ss.at[s, dz - 1], recv_sem=z_rs.at[s, dz - 1],
                device_id=h_peer[dz - 1], device_id_type=MESH,
            )
            c.start()
            h_copies.append(c)
        take_edges(e2)

        def smooth_tile(at):
            weight = jnp.concatenate([keep[at, :]] * 2, axis=1)
            fix[at, :] = weight * fix[at, :] + 0.5 * mm(place[at, :], beside(e2))

        tiles(smooth_tile)
        for c in h_copies:
            c.wait_recv()
        for d in range(3):
            sol = sol + zrecv[s, d].astype(F32)
        sol = sol.astype(BF)

        def update_tile(at):
            value = u[at, :] + OMEGA * (fix[at, :] + mm(b2[at, :], sol))
            u[at, :] = value
            ub[at, :] = value.astype(BF)

        tiles(update_tile)

        for j in range(2):
            @pl.when(leaves[j])
            def _():
                crossings[j].wait_send()
        for c in y_copies + p_copies + x_copies + h_copies:
            c.wait_send()
        for k in range(4):
            @pl.when(present[k])
            def _():
                edge_copy(e1, k).wait_send()
                edge_copy(e2, k).wait_send()
                product_copy(s, k, k ^ 1).wait_send()
                if s == 0:
                    basis_copy(k, k ^ 1).wait_send()

    done = pltpu.make_async_copy(u, out_h.at[0, 0], out_sem)
    done.start()
    done.wait()


def body(load, guess, interface_op, precond, basis, coarse_inverse, edge_rows, coarse_slot):
    ni, cases = load.shape[2:]
    nb = basis.shape[3]
    dma = pltpu.SemaphoreType.DMA
    vm = pltpu.VMEM
    anywhere = pl.BlockSpec(memory_space=pltpu.HBM)
    return pl.pallas_call(
        kernel,
        out_shape=jax.ShapeDtypeStruct(load.shape, F32),
        in_specs=[anywhere] * 8,
        out_specs=anywhere,
        scratch_shapes=[
            vm((ni, cases), F32), vm((ni, cases), F32),
            vm((ni, ni), BF), vm((ni, ni), BF), vm((ni, ni), BF),
            vm((nb, ni), BF), vm((1, ni), jnp.int32), vm((1, nb), jnp.int32),
            vm((ni, ni), BF), vm((ni, ni), BF), vm((ni, nb), BF), vm((nb, ni), BF),
            vm((ni, 128), F32), vm((ni, cases), BF), vm((ni, cases), F32),
            vm((ni, cases), BF), vm((ni, cases), F32),
            vm((2 * ITERS, 4, ni // 4, cases), BF), vm((2 * ITERS, 4, ni // 4, cases), BF),
            vm((4, nb, ni // 4), BF), vm((4, nb, ni // 4), BF),
            vm((ITERS, 4, nb, cases), BF), vm((ITERS, 4, nb, cases), BF),
            vm((ITERS, nb, cases), BF), vm((ITERS, 2, 4, 2, nb, cases), BF),
            vm((ITERS, 3, 4, nb, cases), BF), vm((4, nb, cases), F32),
            vm((ITERS, 3, 4, nb, cases), BF),
            vm((ITERS, 3, nb, cases), BF), vm((ITERS, 3, nb, cases), BF),
            dma((8,)), dma,
            dma((2 * ITERS, 4)), dma((2 * ITERS, 4)),
            dma((4,)), dma((4,)),
            dma((ITERS, 4)), dma((ITERS, 4)),
            dma((ITERS, 2)), dma((ITERS, 2)),
            dma((ITERS, 3)), dma((ITERS, 3)),
            dma((ITERS, 4)), dma((ITERS, 4)),
            dma((ITERS, 3, 4)), dma((ITERS, 3, 4)),
            dma((ITERS, 3)), dma((ITERS, 3)),
        ],
        compiler_params=pltpu.CompilerParams(
            collective_id=0, has_side_effects=True, vmem_limit_bytes=60 * 1024 * 1024
        ),
    )(load, guess, interface_op, precond, basis[0, 0].T, coarse_inverse, edge_rows, coarse_slot)


def solution(mesh):
    cells = (("grp", "row"), "col")
    return jax.shard_map(
        body,
        mesh=mesh,
        in_specs=(
            P(*cells, None, None),
            P(*cells, None, None),
            P(*cells, None, None),
            P(*cells, None, None),
            P(*cells, None, None),
            P(*cells),
            P(*cells, None),
            P(*cells, None),
        ),
        out_specs=P(*cells, None, None),
        check_vma=False,
    )
```

```python
import jax
import jax.numpy as jnp
from jax import lax
from jax.experimental import pallas as pl
from jax.experimental.pallas import tpu as pltpu
from jax.sharding import PartitionSpec as P

ITERS = 2
OMEGA = 0.6
MESH = pl.DeviceIdType.MESH
BF = jnp.bfloat16
F32 = jnp.float32
TILE = 256


def mm(left, right):
    return jnp.dot(left, right, preferred_element_type=F32)


def kernel(
    load_h, guess_h, op_h, pre_h, basis_h, coarse_h, rows_h, slot_h, out_h,
    u, load, amat, mmat, cmat, basis, rows, slot,
    pick, place, b2, b2t, keep, ub, applied, resid, fix,
    pa, mplace, bedge, cown, esend, erecv, cres, gath, ypart, yown, xrecv, zpart, zrecv,
    in_sem, out_sem, e_ss, e_rs, t_ss, t_rs, y_ss, y_rs, p_ss, p_rs, x_ss, x_rs, z_ss, z_rs,
):
    core = lax.axis_index("grp")
    row = lax.axis_index("row")
    col = lax.axis_index("col")
    y, zl = row // 2, lax.rem(row, 2)
    x, zh = col // 4, lax.rem(col, 4)
    a = core * 8 + row
    n_basis = basis.shape[0]

    def at_row(r, c):
        return {"grp": r // 8, "row": lax.rem(r, 8), "col": c}

    loads = [
        pltpu.make_async_copy(src, dst, in_sem.at[i])
        for i, (src, dst) in enumerate(
            [
                (rows_h.at[0], rows),
                (guess_h.at[0, 0], u),
                (op_h.at[0, 0], amat),
                (load_h.at[0, 0], load),
                (slot_h.at[0], slot),
                (basis_h, basis),
                (pre_h.at[0, 0], mmat),
                (coarse_h, cmat),
            ]
        )
    ]
    for c in loads:
        c.start()
    l_rows, l_u, l_a, l_load, l_slot, l_basis, l_m, l_c = loads

    present = [col > 0, col < 15, a > 0, a < 15]
    across = [at_row(a, col - 1), at_row(a, col + 1), at_row(a - 1, col), at_row(a + 1, col)]
    stays = [jnp.logical_and(a == col, zl == j) for j in range(2)]
    mirror = [at_row(col // 2 * 2 + j, a) for j in range(2)]
    y_peer = [{"grp": core, "row": lax.rem(y + d, 4) * 2 + zl, "col": col} for d in (1, 2, 3)]
    c_pair = {"grp": 1 - core, "row": row, "col": col}
    x_peer = [{"grp": core, "row": row, "col": lax.rem(x + d, 4) * 4 + zh} for d in (1, 2, 3)]
    h_peer = [{"grp": core, "row": row, "col": x * 4 + lax.rem(zh + d, 4)} for d in (1, 2, 3)]

    barrier = pltpu.get_barrier_semaphore()
    fixed = y_peer + [c_pair] + x_peer + h_peer
    leaves = [jnp.logical_not(p) for p in stays]
    source = [at_row(col, a // 2 * 2 + j) for j in range(2)]
    for peer in fixed:
        pl.semaphore_signal(barrier, inc=1, device_id=peer, device_id_type=MESH)
    for ok, peer in zip(present + leaves, across + source):
        @pl.when(ok)
        def _():
            pl.semaphore_signal(barrier, inc=1, device_id=peer, device_id_type=MESH)

    for k in range(4):
        @pl.when(jnp.logical_not(present[k]))
        def _():
            for e in range(2 * ITERS):
                erecv[e, k] = jnp.zeros(erecv.shape[2:], BF)

    l_rows.wait()
    ni = pick.shape[0]

    @pl.loop(0, ni // 128)
    def _(t):
        base = pl.multiple_of(t * 128, 128)
        here = rows[:, pl.ds(base, 128)].astype(F32)
        down = jnp.broadcast_to(here, (128, 128)).T.astype(jnp.int32)
        lane = lax.broadcasted_iota(jnp.int32, (128, 128), 1)
        for v in range(ni // 128):
            pick[pl.ds(base, 128), v * 128:(v + 1) * 128] = jnp.where(
                down == lane + v * 128, 1.0, 0.0
            ).astype(BF)
        sub = lax.broadcasted_iota(jnp.int32, (128, ni), 0) + base
        place[pl.ds(base, 128), :] = jnp.where(sub == rows[...], 1.0, 0.0).astype(BF)

    def tiles(body):
        for t in range(ni // TILE):
            body(pl.ds(t * TILE, TILE))

    l_u.wait()
    ub[...] = u[...].astype(BF)

    l_a.wait()

    def edge_copy(e, k):
        return pltpu.make_async_remote_copy(
            src_ref=esend.at[e, k], dst_ref=erecv.at[e, k ^ 1],
            send_sem=e_ss.at[e, k], recv_sem=e_rs.at[e, k ^ 1],
            device_id=across[k], device_id_type=MESH,
        )

    def edge_arrival(e, k):
        return pltpu.make_async_remote_copy(
            src_ref=esend.at[e, k], dst_ref=erecv.at[e, k],
            send_sem=e_ss.at[e, k], recv_sem=e_rs.at[e, k],
            device_id=across[k], device_id_type=MESH,
        )

    def start_edge(e, k):
        @pl.when(present[k])
        def _():
            edge_copy(e, k).start()

    def send_edges(e, source):
        for k in (0, 1, 2, 3):
            esend[e, k] = mm(pick[k * TILE:(k + 1) * TILE, :], source).astype(BF)

            start_edge(e, k)

    def take_edges(e):
        for k in range(4):
            @pl.when(present[k])
            def _():
                edge_arrival(e, k).wait_recv()

    def beside(e):
        return erecv[e].reshape(ni, erecv.shape[3])

    def prepare():
        flag = jnp.concatenate(
            [jnp.full((TILE, 128), p.astype(F32)) for p in present], axis=0
        ).astype(BF)

        def keep_tile(at):
            keep[at, :] = 1.0 - 0.5 * mm(place[at, :], flag)

        tiles(keep_tile)

        l_slot.wait()
        l_basis.wait()
        order = (lax.broadcasted_iota(jnp.int32, (n_basis, n_basis), 0) == slot[...])
        order = jnp.where(order, 1.0, 0.0).astype(BF)
        ordered = mm(order, basis[...])
        b2t[...] = ordered.astype(BF)
        b2[...] = ordered.T.astype(BF)
        bedge[...] = mm(b2t[...], place[...]).astype(BF)
        l_m.wait()

        @pl.loop(0, ni // TILE)
        def _(t):
            at = pl.ds(pl.multiple_of(t * TILE, TILE), TILE)
            mplace[at, :] = mm(mmat[at, :], place[...]).astype(BF)
            pa[at, :] = mm(pick[at, :], amat[...]).astype(BF)

    outs = []
    for s in range(ITERS):
        e1, e2 = 2 * s, 2 * s + 1

        if s > 0:
            for k in range(4):
                esend[e1, k] = mm(pa[k * TILE:(k + 1) * TILE, :], ub[...]).astype(BF)
                start_edge(e1, k)

        def apply_tile(at):
            value = mm(amat[at, :], ub[...])
            applied[at, :] = value
            if s == 0:
                resid[at, :] = value.astype(BF)

        tiles(apply_tile)
        if s == 0:
            total = len(fixed) + sum(p.astype(jnp.int32) for p in present + leaves)
            pl.semaphore_wait(barrier, total)
            send_edges(e1, resid[...])
            prepare()
            l_load.wait()

        def own_tile(at):
            resid[at, :] = (load[at, :] - applied[at, :]).astype(BF)

        tiles(own_tile)
        cown[...] = mm(b2t[...], resid[...])

        def own_fix_tile(at):
            fix[at, :] = mm(mmat[at, :], resid[...])

        tiles(own_fix_tile)
        take_edges(e1)

        cres[s] = (cown[...] - mm(bedge[...], beside(e1))).astype(BF)
        slot_of = gath.at[s, col // 8, lax.rem(col, 8) // 2, lax.rem(col, 2)]
        crossings = [
            pltpu.make_async_remote_copy(
                src_ref=cres.at[s], dst_ref=slot_of,
                send_sem=t_ss.at[s, j], recv_sem=t_rs.at[s, lax.rem(col, 2)],
                device_id=mirror[j], device_id_type=MESH,
            )
            for j in range(2)
        ]
        arrivals = [
            pltpu.make_async_remote_copy(
                src_ref=cres.at[s], dst_ref=gath.at[s, core, y, j],
                send_sem=t_ss.at[s, j], recv_sem=t_rs.at[s, j],
                device_id=source[j], device_id_type=MESH,
            )
            for j in range(2)
        ]
        for j in range(2):
            @pl.when(leaves[j])
            def _():
                crossings[j].start()

            @pl.when(stays[j])
            def _():
                gath[s, core, y, j] = cres[s]

        def fix_tile(at):
            value = fix[at, :] - mm(mplace[at, :], beside(e1))
            fix[at, :] = value
            ub[at, :] = value.astype(BF)

        tiles(fix_tile)

        for j in range(2):
            @pl.when(leaves[j])
            def _():
                arrivals[j].wait_recv()

        def gather_copy(i, from_y, sems, peer):
            ref = gath.at[s, core, from_y]
            return pltpu.make_async_remote_copy(
                src_ref=ref, dst_ref=ref,
                send_sem=sems[0].at[s, i], recv_sem=sems[1].at[s, i],
                device_id=peer, device_id_type=MESH,
            )

        y_sems, p_sems = (y_ss, y_rs), (p_ss, p_rs)
        y_copies = [gather_copy(d, y, y_sems, y_peer[d]) for d in range(3)]
        for c in y_copies:
            c.start()
        p_copies = [gather_copy(3, y, p_sems, c_pair)]
        p_copies[0].start()

        send_edges(e2, ub[...])

        for d in (0, 2, 1):
            from_y = lax.rem(y + 3 - d, 4)
            gather_copy(d, from_y, y_sems, y_peer[d]).wait_recv()
            c = gather_copy(d, from_y, p_sems, c_pair)
            c.start()
            p_copies.append(c)
        for d, c in zip((3, 0, 2, 1), p_copies):
            at_y = y if d == 3 else lax.rem(y + 3 - d, 4)
            other = gath.at[s, 1 - core, at_y]
            pltpu.make_async_remote_copy(
                src_ref=other, dst_ref=other,
                send_sem=p_ss.at[s, d], recv_sem=p_rs.at[s, d],
                device_id=c_pair, device_id_type=MESH,
            ).wait_recv()
        if s == 0:
            l_c.wait()
        vec = gath[s].reshape(ni, gath.shape[5])

        def block_of(d):
            to = lax.rem(x + d, 4)
            return mm(cmat[pl.ds(pl.multiple_of(to * TILE, TILE), TILE), :], vec)

        for d in range(3):
            ypart[s, d] = block_of(d + 1).astype(BF).reshape(ypart.shape[2:])

        def x_copy(j, d):
            at_h = lax.rem(zh + (2, 1, 3, 0)[j], 4)
            return pltpu.make_async_remote_copy(
                src_ref=ypart.at[s, d, at_h], dst_ref=xrecv.at[s, d, at_h],
                send_sem=x_ss.at[s, d, j], recv_sem=x_rs.at[s, d, j],
                device_id=x_peer[d], device_id_type=MESH,
            )

        x_copies = [x_copy(j, d) for j in range(4) for d in (1, 0, 2)]
        for c in x_copies:
            c.start()
        yown[...] = block_of(0).reshape(yown.shape)
        h_copies = []
        for j in range(4):
            dz = (2, 1, 3, 0)[j]
            at_h = lax.rem(zh + dz, 4)
            for c in x_copies[3 * j:3 * j + 3]:
                c.wait_recv()
            part = yown[at_h]
            for d in range(3):
                part = part + xrecv[s, d, at_h].astype(F32)
            if dz == 0:
                sol = part
                continue
            zpart[s, dz - 1] = part.astype(BF)
            c = pltpu.make_async_remote_copy(
                src_ref=zpart.at[s, dz - 1], dst_ref=zrecv.at[s, dz - 1],
                send_sem=z_ss.at[s, dz - 1], recv_sem=z_rs.at[s, dz - 1],
                device_id=h_peer[dz - 1], device_id_type=MESH,
            )
            c.start()
            h_copies.append(c)
        take_edges(e2)

        def smooth_tile(at):
            weight = jnp.concatenate([keep[at, :]] * 2, axis=1)
            fix[at, :] = weight * fix[at, :] + 0.5 * mm(place[at, :], beside(e2))

        tiles(smooth_tile)
        for c in h_copies:
            c.wait_recv()
        for d in range(3):
            sol = sol + zrecv[s, d].astype(F32)
        sol = sol.astype(BF)

        def update_tile(at):
            value = u[at, :] + OMEGA * (fix[at, :] + mm(b2[at, :], sol))
            u[at, :] = value
            if s < ITERS - 1:
                ub[at, :] = value.astype(BF)
            else:
                c = pltpu.make_async_copy(
                    u.at[at], out_h.at[0, 0, at], out_sem.at[len(outs)]
                )
                c.start()
                outs.append(c)

        tiles(update_tile)

        for j in range(2):
            @pl.when(leaves[j])
            def _():
                crossings[j].wait_send()
        for c in y_copies + p_copies + x_copies + h_copies:
            c.wait_send()
        for e in (e1, e2):
            for k in range(4):
                @pl.when(present[k])
                def _():
                    edge_copy(e, k).wait_send()

    for c in outs:
        c.wait()


def body(load, guess, interface_op, precond, basis, coarse_inverse, edge_rows, coarse_slot):
    ni, cases = load.shape[2:]
    nb = basis.shape[3]
    dma = pltpu.SemaphoreType.DMA
    vm = pltpu.VMEM
    anywhere = pl.BlockSpec(memory_space=pltpu.HBM)
    return pl.pallas_call(
        kernel,
        out_shape=jax.ShapeDtypeStruct(load.shape, F32),
        in_specs=[anywhere] * 8,
        out_specs=anywhere,
        scratch_shapes=[
            vm((ni, cases), F32), vm((ni, cases), F32),
            vm((ni, ni), BF), vm((ni, ni), BF), vm((ni, ni), BF),
            vm((nb, ni), BF), vm((1, ni), jnp.int32), vm((1, nb), jnp.int32),
            vm((ni, ni), BF), vm((ni, ni), BF), vm((ni, nb), BF), vm((nb, ni), BF),
            vm((ni, 128), F32), vm((ni, cases), BF), vm((ni, cases), F32),
            vm((ni, cases), BF), vm((ni, cases), F32),
            vm((ni, ni), BF), vm((ni, ni), BF), vm((nb, ni), BF), vm((nb, cases), F32),
            vm((2 * ITERS, 4, ni // 4, cases), BF), vm((2 * ITERS, 4, ni // 4, cases), BF),
            vm((ITERS, nb, cases), BF), vm((ITERS, 2, 4, 2, nb, cases), BF),
            vm((ITERS, 3, 4, nb, cases), BF), vm((4, nb, cases), F32),
            vm((ITERS, 3, 4, nb, cases), BF),
            vm((ITERS, 3, nb, cases), BF), vm((ITERS, 3, nb, cases), BF),
            dma((8,)), dma((4,)),
            dma((2 * ITERS, 4)), dma((2 * ITERS, 4)),
            dma((ITERS, 2)), dma((ITERS, 2)),
            dma((ITERS, 3)), dma((ITERS, 3)),
            dma((ITERS, 4)), dma((ITERS, 4)),
            dma((ITERS, 3, 4)), dma((ITERS, 3, 4)),
            dma((ITERS, 3)), dma((ITERS, 3)),
        ],
        compiler_params=pltpu.CompilerParams(
            collective_id=0, has_side_effects=True, vmem_limit_bytes=60 * 1024 * 1024
        ),
    )(load, guess, interface_op, precond, basis[0, 0].T, coarse_inverse, edge_rows, coarse_slot)


def solution(mesh):
    cells = (("grp", "row"), "col")
    return jax.shard_map(
        body,
        mesh=mesh,
        in_specs=(
            P(*cells, None, None),
            P(*cells, None, None),
            P(*cells, None, None),
            P(*cells, None, None),
            P(*cells, None, None),
            P(*cells),
            P(*cells, None),
            P(*cells, None),
        ),
        out_specs=P(*cells, None, None),
        check_vma=False,
    )
```

```python
import jax
import jax.numpy as jnp
from jax import lax
from jax.experimental import pallas as pl
from jax.experimental.pallas import tpu as pltpu
from jax.sharding import PartitionSpec as P

ITERS = 2
OMEGA = 0.6
MESH = pl.DeviceIdType.MESH
BF = jnp.bfloat16
F32 = jnp.float32
TILE = 256


def mm(left, right):
    return jnp.dot(left, right, preferred_element_type=F32)


def kernel(
    load_h, guess_h, op_h, pre_h, basis_h, coarse_h, rows_h, slot_h, out_h,
    u, load, amat, mmat, cmat, basis, rows, slot,
    pick, place, b2, b2t, keep, ub, applied, resid, fix,
    pa, pab, mplace, bedge, cown, yhalf, esend, erecv, cres, gath, ypart, yown, xrecv, zpart, zrecv,
    in_sem, out_sem, e_ss, e_rs, t_ss, t_rs, y_ss, y_rs, p_ss, p_rs, x_ss, x_rs, z_ss, z_rs,
):
    core = lax.axis_index("grp")
    row = lax.axis_index("row")
    col = lax.axis_index("col")
    y, zl = row // 2, lax.rem(row, 2)
    x, zh = col // 4, lax.rem(col, 4)
    a = core * 8 + row
    n_basis = basis.shape[0]

    def at_row(r, c):
        return {"grp": r // 8, "row": lax.rem(r, 8), "col": c}

    loads = [
        pltpu.make_async_copy(src, dst, in_sem.at[i])
        for i, (src, dst) in enumerate(
            [
                (rows_h.at[0], rows),
                (guess_h.at[0, 0], u),
                (op_h.at[0, 0], amat),
                (load_h.at[0, 0], load),
                (slot_h.at[0], slot),
                (basis_h, basis),
                (pre_h.at[0, 0], mmat),
                (coarse_h, cmat),
            ]
        )
    ]
    for c in loads:
        c.start()
    l_rows, l_u, l_a, l_load, l_slot, l_basis, l_m, l_c = loads

    present = [col > 0, col < 15, a > 0, a < 15]
    across = [at_row(a, col - 1), at_row(a, col + 1), at_row(a - 1, col), at_row(a + 1, col)]
    stays = [jnp.logical_and(a == col, zl == j) for j in range(2)]
    mirror = [at_row(col // 2 * 2 + j, a) for j in range(2)]
    y_peer = [{"grp": core, "row": lax.rem(y + d, 4) * 2 + zl, "col": col} for d in (1, 2, 3)]
    c_pair = {"grp": 1 - core, "row": row, "col": col}
    x_peer = [{"grp": core, "row": row, "col": lax.rem(x + d, 4) * 4 + zh} for d in (1, 2, 3)]
    h_peer = [{"grp": core, "row": row, "col": x * 4 + lax.rem(zh + d, 4)} for d in (1, 2, 3)]

    barrier = pltpu.get_barrier_semaphore()
    fixed = y_peer + [c_pair] + x_peer + h_peer
    leaves = [jnp.logical_not(p) for p in stays]
    source = [at_row(col, a // 2 * 2 + j) for j in range(2)]
    for peer in fixed:
        pl.semaphore_signal(barrier, inc=1, device_id=peer, device_id_type=MESH)
    for ok, peer in zip(present + leaves, across + source):
        @pl.when(ok)
        def _():
            pl.semaphore_signal(barrier, inc=1, device_id=peer, device_id_type=MESH)

    for k in range(4):
        @pl.when(jnp.logical_not(present[k]))
        def _():
            for e in range(2 * ITERS):
                erecv[e, k] = jnp.zeros(erecv.shape[2:], BF)

    l_rows.wait()
    ni = pick.shape[0]

    @pl.loop(0, ni // 128)
    def _(t):
        base = pl.multiple_of(t * 128, 128)
        here = rows[:, pl.ds(base, 128)].astype(F32)
        down = jnp.broadcast_to(here, (128, 128)).T.astype(jnp.int32)
        lane = lax.broadcasted_iota(jnp.int32, (128, 128), 1)
        for v in range(ni // 128):
            pick[pl.ds(base, 128), v * 128:(v + 1) * 128] = jnp.where(
                down == lane + v * 128, 1.0, 0.0
            ).astype(BF)
        sub = lax.broadcasted_iota(jnp.int32, (128, ni), 0) + base
        place[pl.ds(base, 128), :] = jnp.where(sub == rows[...], 1.0, 0.0).astype(BF)

    def tiles(body):
        for t in range(ni // TILE):
            body(pl.ds(t * TILE, TILE))

    l_u.wait()
    ub[...] = u[...].astype(BF)

    l_a.wait()

    def edge_copy(e, k):
        return pltpu.make_async_remote_copy(
            src_ref=esend.at[e, k], dst_ref=erecv.at[e, k ^ 1],
            send_sem=e_ss.at[e, k], recv_sem=e_rs.at[e, k ^ 1],
            device_id=across[k], device_id_type=MESH,
        )

    def edge_arrival(e, k):
        return pltpu.make_async_remote_copy(
            src_ref=esend.at[e, k], dst_ref=erecv.at[e, k],
            send_sem=e_ss.at[e, k], recv_sem=e_rs.at[e, k],
            device_id=across[k], device_id_type=MESH,
        )

    def start_edge(e, k):
        @pl.when(present[k])
        def _():
            edge_copy(e, k).start()

    def send_edges(e, source):
        for k in (0, 1, 2, 3):
            esend[e, k] = mm(pick[k * TILE:(k + 1) * TILE, :], source).astype(BF)

            start_edge(e, k)

    def take_edges(e):
        for k in range(4):
            @pl.when(present[k])
            def _():
                edge_arrival(e, k).wait_recv()

    def beside(e):
        return erecv[e].reshape(ni, erecv.shape[3])

    def prepare():
        flag = jnp.concatenate(
            [jnp.full((TILE, 128), p.astype(F32)) for p in present], axis=0
        ).astype(BF)

        def keep_tile(at):
            keep[at, :] = 1.0 - 0.5 * mm(place[at, :], flag)

        tiles(keep_tile)

        l_slot.wait()
        l_basis.wait()
        order = (lax.broadcasted_iota(jnp.int32, (n_basis, n_basis), 0) == slot[...])
        order = jnp.where(order, 1.0, 0.0).astype(BF)
        ordered = mm(order, basis[...])
        b2t[...] = ordered.astype(BF)
        b2[...] = ordered.T.astype(BF)
        bedge[...] = mm(b2t[...], place[...]).astype(BF)
        l_m.wait()

        @pl.loop(0, ni // TILE)
        def _(t):
            across_at = pl.ds(pl.multiple_of(t * TILE, TILE), TILE)
            mplace[:, across_at] = mm(mmat[...], place[:, across_at]).astype(BF)
            pa[:, across_at] = mm(pick[...], amat[:, across_at]).astype(BF)
        pab[...] = mm(pa[...], b2[...]).astype(BF)

    outs = []
    for s in range(ITERS):
        e1, e2 = 2 * s, 2 * s + 1

        def apply_tile(at):
            value = mm(amat[at, :], ub[...])
            applied[at, :] = value
            if s == 0:
                resid[at, :] = value.astype(BF)

        tiles(apply_tile)
        if s == 0:
            total = len(fixed) + sum(p.astype(jnp.int32) for p in present + leaves)
            pl.semaphore_wait(barrier, total)
            send_edges(e1, resid[...])
            prepare()
            l_load.wait()

        def own_tile(at):
            resid[at, :] = (load[at, :] - applied[at, :]).astype(BF)

        tiles(own_tile)
        cown[...] = mm(b2t[...], resid[...])

        def own_fix_tile(at):
            fix[at, :] = mm(mmat[at, :], resid[...])

        tiles(own_fix_tile)
        take_edges(e1)

        cres[s] = (cown[...] - mm(bedge[...], beside(e1))).astype(BF)
        slot_of = gath.at[s, col // 8, lax.rem(col, 8) // 2, lax.rem(col, 2)]
        crossings = [
            pltpu.make_async_remote_copy(
                src_ref=cres.at[s], dst_ref=slot_of,
                send_sem=t_ss.at[s, j], recv_sem=t_rs.at[s, lax.rem(col, 2)],
                device_id=mirror[j], device_id_type=MESH,
            )
            for j in range(2)
        ]
        arrivals = [
            pltpu.make_async_remote_copy(
                src_ref=cres.at[s], dst_ref=gath.at[s, core, y, j],
                send_sem=t_ss.at[s, j], recv_sem=t_rs.at[s, j],
                device_id=source[j], device_id_type=MESH,
            )
            for j in range(2)
        ]
        for j in range(2):
            @pl.when(leaves[j])
            def _():
                crossings[j].start()

            @pl.when(stays[j])
            def _():
                gath[s, core, y, j] = cres[s]

        def fix_tile(at):
            value = fix[at, :] - mm(mplace[at, :], beside(e1))
            fix[at, :] = value
            ub[at, :] = value.astype(BF)

        tiles(fix_tile)

        for j in range(2):
            @pl.when(leaves[j])
            def _():
                arrivals[j].wait_recv()

        def gather_copy(i, from_y, sems, peer):
            ref = gath.at[s, core, from_y]
            return pltpu.make_async_remote_copy(
                src_ref=ref, dst_ref=ref,
                send_sem=sems[0].at[s, i], recv_sem=sems[1].at[s, i],
                device_id=peer, device_id_type=MESH,
            )

        y_sems, p_sems = (y_ss, y_rs), (p_ss, p_rs)
        y_copies = [gather_copy(d, y, y_sems, y_peer[d]) for d in range(3)]
        for c in y_copies:
            c.start()
        p_copies = [gather_copy(3, y, p_sems, c_pair)]
        p_copies[0].start()

        send_edges(e2, ub[...])

        for d in (0, 2, 1):
            from_y = lax.rem(y + 3 - d, 4)
            gather_copy(d, from_y, y_sems, y_peer[d]).wait_recv()
            c = gather_copy(d, from_y, p_sems, c_pair)
            c.start()
            p_copies.append(c)
        if s == 0:
            l_c.wait()
        span = ni // 2
        own_at = pl.ds(pl.multiple_of(core * span, span), span)
        other_at = pl.ds(pl.multiple_of((1 - core) * span, span), span)
        ready = gath[s, core].reshape(span, gath.shape[5])
        for k in range(4):
            yhalf[k] = mm(cmat[k * TILE:(k + 1) * TILE, own_at], ready)
        for d, c in zip((3, 0, 2, 1), p_copies):
            at_y = y if d == 3 else lax.rem(y + 3 - d, 4)
            other = gath.at[s, 1 - core, at_y]
            pltpu.make_async_remote_copy(
                src_ref=other, dst_ref=other,
                send_sem=p_ss.at[s, d], recv_sem=p_rs.at[s, d],
                device_id=c_pair, device_id_type=MESH,
            ).wait_recv()
        vec = gath[s, 1 - core].reshape(span, gath.shape[5])

        def block_of(d):
            to = lax.rem(x + d, 4)
            at = pl.ds(pl.multiple_of(to * TILE, TILE), TILE)
            return yhalf[to] + mm(cmat[at, other_at], vec)

        for d in range(3):
            ypart[s, d] = block_of(d + 1).astype(BF).reshape(ypart.shape[2:])

        def x_copy(j, d):
            at_h = lax.rem(zh + (2, 1, 3, 0)[j], 4)
            return pltpu.make_async_remote_copy(
                src_ref=ypart.at[s, d, at_h], dst_ref=xrecv.at[s, d, at_h],
                send_sem=x_ss.at[s, d, j], recv_sem=x_rs.at[s, d, j],
                device_id=x_peer[d], device_id_type=MESH,
            )

        x_copies = [x_copy(j, d) for j in range(4) for d in (1, 0, 2)]
        for c in x_copies:
            c.start()
        yown[...] = block_of(0).reshape(yown.shape)
        h_copies = []
        for j in range(4):
            dz = (2, 1, 3, 0)[j]
            at_h = lax.rem(zh + dz, 4)
            for c in x_copies[3 * j:3 * j + 3]:
                c.wait_recv()
            part = yown[at_h]
            for d in range(3):
                part = part + xrecv[s, d, at_h].astype(F32)
            if dz == 0:
                sol = part
                continue
            zpart[s, dz - 1] = part.astype(BF)
            c = pltpu.make_async_remote_copy(
                src_ref=zpart.at[s, dz - 1], dst_ref=zrecv.at[s, dz - 1],
                send_sem=z_ss.at[s, dz - 1], recv_sem=z_rs.at[s, dz - 1],
                device_id=h_peer[dz - 1], device_id_type=MESH,
            )
            c.start()
            h_copies.append(c)
        take_edges(e2)

        def smooth_tile(at):
            weight = jnp.concatenate([keep[at, :]] * 2, axis=1)
            fix[at, :] = weight * fix[at, :] + 0.5 * mm(place[at, :], beside(e2))

        tiles(smooth_tile)
        if s < ITERS - 1:
            def ahead_tile(at):
                ub[at, :] = (u[at, :] + OMEGA * fix[at, :]).astype(BF)

            def ahead_edge(at):
                applied[at, :] = mm(pa[at, :], ub[...])

            tiles(ahead_tile)
            tiles(ahead_edge)
        for c in h_copies:
            c.wait_recv()
        for d in range(3):
            sol = sol + zrecv[s, d].astype(F32)
        sol = sol.astype(BF)

        if s < ITERS - 1:
            for k in range(4):
                at = slice(k * TILE, (k + 1) * TILE)
                value = applied[at, :] + OMEGA * mm(pab[at, :], sol)
                esend[e1 + 2, k] = value.astype(BF)
                start_edge(e1 + 2, k)

        def update_tile(at):
            value = u[at, :] + OMEGA * (fix[at, :] + mm(b2[at, :], sol))
            u[at, :] = value
            if s < ITERS - 1:
                ub[at, :] = value.astype(BF)
            else:
                c = pltpu.make_async_copy(
                    u.at[at], out_h.at[0, 0, at], out_sem.at[len(outs)]
                )
                c.start()
                outs.append(c)

        tiles(update_tile)

        for j in range(2):
            @pl.when(leaves[j])
            def _():
                crossings[j].wait_send()
        for c in y_copies + p_copies + x_copies + h_copies:
            c.wait_send()
        for e in (e1, e2):
            for k in range(4):
                @pl.when(present[k])
                def _():
                    edge_copy(e, k).wait_send()

    for c in outs:
        c.wait()


def body(load, guess, interface_op, precond, basis, coarse_inverse, edge_rows, coarse_slot):
    ni, cases = load.shape[2:]
    nb = basis.shape[3]
    dma = pltpu.SemaphoreType.DMA
    vm = pltpu.VMEM
    anywhere = pl.BlockSpec(memory_space=pltpu.HBM)
    return pl.pallas_call(
        kernel,
        out_shape=jax.ShapeDtypeStruct(load.shape, F32),
        in_specs=[anywhere] * 8,
        out_specs=anywhere,
        scratch_shapes=[
            vm((ni, cases), F32), vm((ni, cases), F32),
            vm((ni, ni), BF), vm((ni, ni), BF), vm((ni, ni), BF),
            vm((nb, ni), BF), vm((1, ni), jnp.int32), vm((1, nb), jnp.int32),
            vm((ni, ni), BF), vm((ni, ni), BF), vm((ni, nb), BF), vm((nb, ni), BF),
            vm((ni, 128), F32), vm((ni, cases), BF), vm((ni, cases), F32),
            vm((ni, cases), BF), vm((ni, cases), F32),
            vm((ni, ni), BF), vm((ni, nb), BF), vm((ni, ni), BF), vm((nb, ni), BF), vm((nb, cases), F32),
            vm((4, TILE, cases), F32),
            vm((2 * ITERS, 4, ni // 4, cases), BF), vm((2 * ITERS, 4, ni // 4, cases), BF),
            vm((ITERS, nb, cases), BF), vm((ITERS, 2, 4, 2, nb, cases), BF),
            vm((ITERS, 3, 4, nb, cases), BF), vm((4, nb, cases), F32),
            vm((ITERS, 3, 4, nb, cases), BF),
            vm((ITERS, 3, nb, cases), BF), vm((ITERS, 3, nb, cases), BF),
            dma((8,)), dma((4,)),
            dma((2 * ITERS, 4)), dma((2 * ITERS, 4)),
            dma((ITERS, 2)), dma((ITERS, 2)),
            dma((ITERS, 3)), dma((ITERS, 3)),
            dma((ITERS, 4)), dma((ITERS, 4)),
            dma((ITERS, 3, 4)), dma((ITERS, 3, 4)),
            dma((ITERS, 3)), dma((ITERS, 3)),
        ],
        compiler_params=pltpu.CompilerParams(
            collective_id=0, has_side_effects=True, vmem_limit_bytes=60 * 1024 * 1024
        ),
    )(load, guess, interface_op, precond, basis[0, 0].T, coarse_inverse, edge_rows, coarse_slot)


def solution(mesh):
    cells = (("grp", "row"), "col")
    return jax.shard_map(
        body,
        mesh=mesh,
        in_specs=(
            P(*cells, None, None),
            P(*cells, None, None),
            P(*cells, None, None),
            P(*cells, None, None),
            P(*cells, None, None),
            P(*cells),
            P(*cells, None),
            P(*cells, None),
        ),
        out_specs=P(*cells, None, None),
        check_vma=False,
    )
```

```python
import jax
import jax.numpy as jnp
from jax import lax
from jax.experimental import pallas as pl
from jax.experimental.pallas import tpu as pltpu
from jax.sharding import PartitionSpec as P

ITERS = 2
OMEGA = 0.6
MESH = pl.DeviceIdType.MESH
BF = jnp.bfloat16
F32 = jnp.float32
TILE = 256


def mm(left, right):
    return jnp.dot(left, right, preferred_element_type=F32)


def kernel(
    load_h, guess_h, op_h, pre_h, basis_h, coarse_h, rows_h, slot_h, out_h,
    u, load, amat, mmat, cmat, basis, rows, slot,
    pick, place, b2, b2t, keep, ub, applied, resid, fix,
    pa, pab, mplace, bedge, cown, yhalf, esend, erecv, cres, gath, ypart, yown, xrecv, zpart, zrecv,
    in_sem, out_sem, e_ss, e_rs, t_ss, t_rs, y_ss, y_rs, p_ss, p_rs, x_ss, x_rs, z_ss, z_rs,
):
    core = lax.axis_index("grp")
    row = lax.axis_index("row")
    col = lax.axis_index("col")
    y, zl = row // 2, lax.rem(row, 2)
    x, zh = col // 4, lax.rem(col, 4)
    a = core * 8 + row
    n_basis = basis.shape[0]

    def at_row(r, c):
        return {"grp": r // 8, "row": lax.rem(r, 8), "col": c}

    loads = [
        pltpu.make_async_copy(src, dst, in_sem.at[i])
        for i, (src, dst) in enumerate(
            [
                (rows_h.at[0], rows),
                (guess_h.at[0, 0], u),
                (op_h.at[0, 0], amat),
                (load_h.at[0, 0], load),
                (slot_h.at[0], slot),
                (basis_h, basis),
                (pre_h.at[0, 0], mmat),
                (coarse_h, cmat),
            ]
        )
    ]
    for c in loads:
        c.start()
    l_rows, l_u, l_a, l_load, l_slot, l_basis, l_m, l_c = loads

    present = [col > 0, col < 15, a > 0, a < 15]
    across = [at_row(a, col - 1), at_row(a, col + 1), at_row(a - 1, col), at_row(a + 1, col)]
    stays = [jnp.logical_and(a == col, zl == j) for j in range(2)]
    mirror = [at_row(col // 2 * 2 + j, a) for j in range(2)]
    y_peer = [{"grp": core, "row": lax.rem(y + d, 4) * 2 + zl, "col": col} for d in (1, 2, 3)]
    c_pair = {"grp": 1 - core, "row": row, "col": col}
    x_peer = [{"grp": core, "row": row, "col": lax.rem(x + d, 4) * 4 + zh} for d in (1, 2, 3)]
    h_peer = [{"grp": core, "row": row, "col": x * 4 + lax.rem(zh + d, 4)} for d in (1, 2, 3)]

    barrier = pltpu.get_barrier_semaphore()
    fixed = y_peer + [c_pair] + x_peer + h_peer
    leaves = [jnp.logical_not(p) for p in stays]
    source = [at_row(col, a // 2 * 2 + j) for j in range(2)]
    for peer in fixed:
        pl.semaphore_signal(barrier, inc=1, device_id=peer, device_id_type=MESH)
    for ok, peer in zip(present + leaves, across + source):
        @pl.when(ok)
        def _():
            pl.semaphore_signal(barrier, inc=1, device_id=peer, device_id_type=MESH)

    for k in range(4):
        @pl.when(jnp.logical_not(present[k]))
        def _():
            for e in range(2 * ITERS):
                erecv[e, k] = jnp.zeros(erecv.shape[2:], BF)

    l_rows.wait()
    ni = pick.shape[0]

    @pl.loop(0, ni // 128)
    def _(t):
        base = pl.multiple_of(t * 128, 128)
        here = rows[:, pl.ds(base, 128)].astype(F32)
        down = jnp.broadcast_to(here, (128, 128)).T.astype(jnp.int32)
        lane = lax.broadcasted_iota(jnp.int32, (128, 128), 1)
        for v in range(ni // 128):
            pick[pl.ds(base, 128), v * 128:(v + 1) * 128] = jnp.where(
                down == lane + v * 128, 1.0, 0.0
            ).astype(BF)
        sub = lax.broadcasted_iota(jnp.int32, (128, ni), 0) + base
        place[pl.ds(base, 128), :] = jnp.where(sub == rows[...], 1.0, 0.0).astype(BF)

    def tiles(body):
        for t in range(ni // TILE):
            body(pl.ds(t * TILE, TILE))

    l_u.wait()
    ub[...] = u[...].astype(BF)

    l_a.wait()

    def edge_copy(e, k):
        return pltpu.make_async_remote_copy(
            src_ref=esend.at[e, k], dst_ref=erecv.at[e, k ^ 1],
            send_sem=e_ss.at[e, k], recv_sem=e_rs.at[e, k ^ 1],
            device_id=across[k], device_id_type=MESH,
        )

    def edge_arrival(e, k):
        return pltpu.make_async_remote_copy(
            src_ref=esend.at[e, k], dst_ref=erecv.at[e, k],
            send_sem=e_ss.at[e, k], recv_sem=e_rs.at[e, k],
            device_id=across[k], device_id_type=MESH,
        )

    def start_edge(e, k):
        @pl.when(present[k])
        def _():
            edge_copy(e, k).start()

    def send_edges(e, source):
        for k in (0, 1, 2, 3):
            esend[e, k] = mm(pick[k * TILE:(k + 1) * TILE, :], source).astype(BF)

            start_edge(e, k)

    def take_edges(e):
        for k in range(4):
            @pl.when(present[k])
            def _():
                edge_arrival(e, k).wait_recv()

    def beside(e):
        return erecv[e].reshape(ni, erecv.shape[3])

    def prepare():
        flag = jnp.concatenate(
            [jnp.full((TILE, 128), p.astype(F32)) for p in present], axis=0
        ).astype(BF)

        def keep_tile(at):
            keep[at, :] = 1.0 - 0.5 * mm(place[at, :], flag)

        tiles(keep_tile)

        l_slot.wait()
        l_basis.wait()
        order = (lax.broadcasted_iota(jnp.int32, (n_basis, n_basis), 0) == slot[...])
        order = jnp.where(order, 1.0, 0.0).astype(BF)
        ordered = mm(order, basis[...])
        b2t[...] = ordered.astype(BF)
        b2[...] = ordered.T.astype(BF)
        bedge[...] = mm(b2t[...], place[...]).astype(BF)
        l_m.wait()

        @pl.loop(0, ni // TILE)
        def _(t):
            at = pl.ds(pl.multiple_of(t * TILE, TILE), TILE)
            mplace[at, :] = mm(mmat[at, :], place[...]).astype(BF)
            pa[at, :] = mm(pick[at, :], amat[...]).astype(BF)
            pab[at, :] = mm(pa[at, :], b2[...]).astype(BF)

    outs = []
    for s in range(ITERS):
        e1, e2 = 2 * s, 2 * s + 1

        def apply_tile(at):
            value = mm(amat[at, :], ub[...])
            applied[at, :] = value
            if s == 0:
                resid[at, :] = value.astype(BF)

        tiles(apply_tile)
        if s == 0:
            total = len(fixed) + sum(p.astype(jnp.int32) for p in present + leaves)
            pl.semaphore_wait(barrier, total)
            send_edges(e1, resid[...])
            prepare()
            l_load.wait()

        def own_tile(at):
            resid[at, :] = (load[at, :] - applied[at, :]).astype(BF)

        tiles(own_tile)
        cown[...] = mm(b2t[...], resid[...])

        def own_fix_tile(at):
            fix[at, :] = mm(mmat[at, :], resid[...])

        tiles(own_fix_tile)
        take_edges(e1)

        cres[s] = (cown[...] - mm(bedge[...], beside(e1))).astype(BF)
        slot_of = gath.at[s, col // 8, lax.rem(col, 8) // 2, lax.rem(col, 2)]
        crossings = [
            pltpu.make_async_remote_copy(
                src_ref=cres.at[s], dst_ref=slot_of,
                send_sem=t_ss.at[s, j], recv_sem=t_rs.at[s, lax.rem(col, 2)],
                device_id=mirror[j], device_id_type=MESH,
            )
            for j in range(2)
        ]
        arrivals = [
            pltpu.make_async_remote_copy(
                src_ref=cres.at[s], dst_ref=gath.at[s, core, y, j],
                send_sem=t_ss.at[s, j], recv_sem=t_rs.at[s, j],
                device_id=source[j], device_id_type=MESH,
            )
            for j in range(2)
        ]
        for j in range(2):
            @pl.when(leaves[j])
            def _():
                crossings[j].start()

            @pl.when(stays[j])
            def _():
                gath[s, core, y, j] = cres[s]

        def fix_tile(at):
            value = fix[at, :] - mm(mplace[at, :], beside(e1))
            fix[at, :] = value
            ub[at, :] = value.astype(BF)

        tiles(fix_tile)

        for j in range(2):
            @pl.when(leaves[j])
            def _():
                arrivals[j].wait_recv()

        def gather_copy(i, from_y, sems, peer):
            ref = gath.at[s, core, from_y]
            return pltpu.make_async_remote_copy(
                src_ref=ref, dst_ref=ref,
                send_sem=sems[0].at[s, i], recv_sem=sems[1].at[s, i],
                device_id=peer, device_id_type=MESH,
            )

        y_sems, p_sems = (y_ss, y_rs), (p_ss, p_rs)
        y_copies = [gather_copy(d, y, y_sems, y_peer[d]) for d in range(3)]
        for c in y_copies:
            c.start()
        p_copies = [gather_copy(3, y, p_sems, c_pair)]
        p_copies[0].start()

        send_edges(e2, ub[...])

        for d in (0, 2, 1):
            from_y = lax.rem(y + 3 - d, 4)
            gather_copy(d, from_y, y_sems, y_peer[d]).wait_recv()
            c = gather_copy(d, from_y, p_sems, c_pair)
            c.start()
            p_copies.append(c)
        if s == 0:
            l_c.wait()
        span = ni // 2
        own_at = pl.ds(pl.multiple_of(core * span, span), span)
        other_at = pl.ds(pl.multiple_of((1 - core) * span, span), span)
        ready = gath[s, core].reshape(span, gath.shape[5])
        for k in range(4):
            yhalf[k] = mm(cmat[k * TILE:(k + 1) * TILE, own_at], ready)
        for d, c in zip((3, 0, 2, 1), p_copies):
            at_y = y if d == 3 else lax.rem(y + 3 - d, 4)
            other = gath.at[s, 1 - core, at_y]
            pltpu.make_async_remote_copy(
                src_ref=other, dst_ref=other,
                send_sem=p_ss.at[s, d], recv_sem=p_rs.at[s, d],
                device_id=c_pair, device_id_type=MESH,
            ).wait_recv()
        vec = gath[s, 1 - core].reshape(span, gath.shape[5])

        def block_of(d):
            to = lax.rem(x + d, 4)
            at = pl.ds(pl.multiple_of(to * TILE, TILE), TILE)
            return yhalf[to] + mm(cmat[at, other_at], vec)

        for d in range(3):
            ypart[s, d] = block_of(d + 1).astype(BF).reshape(ypart.shape[2:])

        def x_copy(j, d):
            at_h = lax.rem(zh + (2, 1, 3, 0)[j], 4)
            return pltpu.make_async_remote_copy(
                src_ref=ypart.at[s, d, at_h], dst_ref=xrecv.at[s, d, at_h],
                send_sem=x_ss.at[s, d, j], recv_sem=x_rs.at[s, d, j],
                device_id=x_peer[d], device_id_type=MESH,
            )

        x_copies = [x_copy(j, d) for j in range(4) for d in (1, 0, 2)]
        for c in x_copies:
            c.start()
        yown[...] = block_of(0).reshape(yown.shape)
        h_copies = []
        for j in range(4):
            dz = (2, 1, 3, 0)[j]
            at_h = lax.rem(zh + dz, 4)
            for c in x_copies[3 * j:3 * j + 3]:
                c.wait_recv()
            part = yown[at_h]
            for d in range(3):
                part = part + xrecv[s, d, at_h].astype(F32)
            if dz == 0:
                sol = part
                continue
            zpart[s, dz - 1] = part.astype(BF)
            c = pltpu.make_async_remote_copy(
                src_ref=zpart.at[s, dz - 1], dst_ref=zrecv.at[s, dz - 1],
                send_sem=z_ss.at[s, dz - 1], recv_sem=z_rs.at[s, dz - 1],
                device_id=h_peer[dz - 1], device_id_type=MESH,
            )
            c.start()
            h_copies.append(c)
        take_edges(e2)

        def smooth_tile(at):
            weight = jnp.concatenate([keep[at, :]] * 2, axis=1)
            fix[at, :] = weight * fix[at, :] + 0.5 * mm(place[at, :], beside(e2))

        tiles(smooth_tile)
        if s < ITERS - 1:
            def ahead_tile(at):
                ub[at, :] = (u[at, :] + OMEGA * fix[at, :]).astype(BF)

            def ahead_edge(at):
                applied[at, :] = mm(pa[at, :], ub[...])

            tiles(ahead_tile)
            tiles(ahead_edge)
        for c in h_copies:
            c.wait_recv()
        for d in range(3):
            sol = sol + zrecv[s, d].astype(F32)
        sol = sol.astype(BF)

        if s < ITERS - 1:
            for k in range(4):
                at = slice(k * TILE, (k + 1) * TILE)
                value = applied[at, :] + OMEGA * mm(pab[at, :], sol)
                esend[e1 + 2, k] = value.astype(BF)
                start_edge(e1 + 2, k)

        def update_tile(at):
            value = u[at, :] + OMEGA * (fix[at, :] + mm(b2[at, :], sol))
            u[at, :] = value
            if s < ITERS - 1:
                ub[at, :] = value.astype(BF)
            else:
                c = pltpu.make_async_copy(
                    u.at[at], out_h.at[0, 0, at], out_sem.at[len(outs)]
                )
                c.start()
                outs.append(c)

        tiles(update_tile)

        for j in range(2):
            @pl.when(leaves[j])
            def _():
                crossings[j].wait_send()
        for c in y_copies + p_copies + x_copies + h_copies:
            c.wait_send()
        for e in (e1, e2):
            for k in range(4):
                @pl.when(present[k])
                def _():
                    edge_copy(e, k).wait_send()

    for c in outs:
        c.wait()


def body(load, guess, interface_op, precond, basis, coarse_inverse, edge_rows, coarse_slot):
    ni, cases = load.shape[2:]
    nb = basis.shape[3]
    dma = pltpu.SemaphoreType.DMA
    vm = pltpu.VMEM
    anywhere = pl.BlockSpec(memory_space=pltpu.HBM)
    return pl.pallas_call(
        kernel,
        out_shape=jax.ShapeDtypeStruct(load.shape, F32),
        in_specs=[anywhere] * 8,
        out_specs=anywhere,
        scratch_shapes=[
            vm((ni, cases), F32), vm((ni, cases), F32),
            vm((ni, ni), BF), vm((ni, ni), BF), vm((ni, ni), BF),
            vm((nb, ni), BF), vm((1, ni), jnp.int32), vm((1, nb), jnp.int32),
            vm((ni, ni), BF), vm((ni, ni), BF), vm((ni, nb), BF), vm((nb, ni), BF),
            vm((ni, 128), F32), vm((ni, cases), BF), vm((ni, cases), F32),
            vm((ni, cases), BF), vm((ni, cases), F32),
            vm((ni, ni), BF), vm((ni, nb), BF), vm((ni, ni), BF), vm((nb, ni), BF), vm((nb, cases), F32),
            vm((4, TILE, cases), F32),
            vm((2 * ITERS, 4, ni // 4, cases), BF), vm((2 * ITERS, 4, ni // 4, cases), BF),
            vm((ITERS, nb, cases), BF), vm((ITERS, 2, 4, 2, nb, cases), BF),
            vm((ITERS, 3, 4, nb, cases), BF), vm((4, nb, cases), F32),
            vm((ITERS, 3, 4, nb, cases), BF),
            vm((ITERS, 3, nb, cases), BF), vm((ITERS, 3, nb, cases), BF),
            dma((8,)), dma((4,)),
            dma((2 * ITERS, 4)), dma((2 * ITERS, 4)),
            dma((ITERS, 2)), dma((ITERS, 2)),
            dma((ITERS, 3)), dma((ITERS, 3)),
            dma((ITERS, 4)), dma((ITERS, 4)),
            dma((ITERS, 3, 4)), dma((ITERS, 3, 4)),
            dma((ITERS, 3)), dma((ITERS, 3)),
        ],
        compiler_params=pltpu.CompilerParams(
            collective_id=0, has_side_effects=True, vmem_limit_bytes=60 * 1024 * 1024
        ),
    )(load, guess, interface_op, precond, basis[0, 0].T, coarse_inverse, edge_rows, coarse_slot)


def solution(mesh):
    cells = (("grp", "row"), "col")
    return jax.shard_map(
        body,
        mesh=mesh,
        in_specs=(
            P(*cells, None, None),
            P(*cells, None, None),
            P(*cells, None, None),
            P(*cells, None, None),
            P(*cells, None, None),
            P(*cells),
            P(*cells, None),
            P(*cells, None),
        ),
        out_specs=P(*cells, None, None),
        check_vma=False,
    )
```
